256 devices in a mesh: dp: 16 (over y, x), context: 16 (over z, core).
Axes of the slice: x: 4, y: 4, z: 8, core: 2. Of those that a mesh axis runs over, the one named last changes fastest.
Arguments:
- query_rows: bfloat16 [16, 3072, 1024], P('dp', 'context'), may hold values from -40 to 40
- key_rows: bfloat16 [16, 3072, 128], P('dp', 'context'), may hold values from -12 to 12
- value_rows: bfloat16 [16, 3072, 128], P('dp', 'context'), may hold values from -6 to 6
- out_grads: bfloat16 [16, 3072, 1024], P('dp', 'context'), may hold values from -16 to 16
- layer_input: bfloat16 [16, 3072, 8192], P('dp', 'context'), may hold values from -6 to 6
- doc_ids: int32 [16, 3072], P('dp'), may hold values from 0 to 7, never falling along the last dimension, each value on 1 to 1536 neighbouring positions
- pair_span: int32 [16], replicated, may hold values from 0 to 15, each once
Outputs:
- grad_qkv: bfloat16 [16, 3072, 1280], P('dp', 'context')
- grad_weight: float32 [8192, 1280], P(('dp', 'context'))
- amax_record: float32 [16, 16, 2], P('dp', 'context')
The draws below stay inside these ranges and needn't reach their ends.
Inputs may be any that keep to these rules, and one draw needn't show every extreme that they name: doc_ids[b] never falls along positions; each document holds 1 to 1536 positions, one exactly 1536. `pair_span`: each of 0 to 15 once.
All inputs are finite; a program needn't handle non-finite values.
Results may differ from the reference program's by a relative error of at most 0.0056.
Values may be sent and summed in bfloat16 or wider, within the bound.
A program may use at most 64 MiB of HBM per device.

```python
import math
import jax
import jax.numpy as jnp
import numpy as np
from jax import lax

D = 8192
H = 8
HD = 128
DOCS = 8
SPAN = 96
PAIRS = 16
LEN = 3072
SEQS = 16
QKV = 1280


def draw_query_rows(key, part):
    drawn = jax.random.truncated_normal(jax.random.fold_in(key, 3), -4.0, 4.0, (SEQS, LEN, H, HD), jnp.float32)
    return drawn.reshape(SEQS, LEN, H * HD).astype(jnp.bfloat16)


def draw_key_rows(key, part):
    drawn = jax.random.truncated_normal(jax.random.fold_in(key, 5), -4.0, 4.0, (SEQS, LEN, HD), jnp.float32)
    return drawn.astype(jnp.bfloat16)


def draw_out_grads(key, part):
    rising = jnp.arange(SEQS * LEN, dtype=jnp.float32).reshape(SEQS, LEN, 1) / (SEQS * LEN)
    noise = jax.random.truncated_normal(jax.random.fold_in(key, 9), -4.0, 4.0, (SEQS, LEN, H * HD), jnp.float32)
    factor = 3.0 ** rising
    return (noise * factor).astype(jnp.bfloat16)


def spiked(values, own_key, source, target, parts, factor):
    owner, partner = [(jnp.arange(values.shape[position]) // (values.shape[position] // parts)).reshape([-1 if axis == position else 1 for axis in range(values.ndim)]) for position in (source, target)]
    chosen = jax.random.permutation(own_key, parts)[partner]
    strong = (owner == chosen) | (owner == (partner + parts // 2) % parts)
    return jnp.where(strong, factor * values, values)


def block_scale(stream_key, dims, split, smallest, largest):
    factor_of = 1.0
    for dim, shards_of in split:
        heights = jax.random.uniform(jax.random.fold_in(jax.random.fold_in(stream_key, 6), dim), (shards_of,), jnp.float32, smallest / len(split), largest / len(split))
        factor_of = factor_of * jnp.repeat(jnp.exp(heights), dims[dim] // shards_of).reshape((-1,) + (1,) * (len(dims) - 1 - dim))
    return factor_of


def length_profile(count, total, most, skew):
    portions = [(1 << 20) // math.isqrt(rank ** skew) + 1 for rank in range(2, count + 1)]
    spare, given = total - most - (count - 1), [1] * (count - 1)
    while spare > 0:
        candidates = [i for i in range(count - 1) if given[i] < most]
        pool, left = sum([portions[i] for i in candidates]), spare
        for i in candidates:
            more = min(most - given[i], max(1, left * portions[i] // pool), spare)
            given[i] = given[i] + more
            spare = spare - more
    return np.array([most] + given)


def uneven(rng, count, total, most, skew):
    if count == 2:
        one = jax.random.randint(rng, (), max(1, total - most), min(most, total - 1) + 1)
        return jnp.stack([one, total - one])
    sizes = jnp.asarray(length_profile(count, total, most, skew), jnp.int32)
    twos = (count - 1) // 2
    donor, receiver = sizes[1:1 + 2 * twos:2], sizes[2:2 + 2 * twos:2]
    slack = jnp.minimum(donor - 1, most - receiver)
    shifted = jax.random.randint(jax.random.fold_in(rng, 1), (twos,), 0, 1 << 20) % (slack + 1)
    sizes = sizes.at[1:1 + 2 * twos:2].set(donor - shifted).at[2:2 + 2 * twos:2].set(receiver + shifted)
    return sizes[jax.random.permutation(jax.random.fold_in(rng, 2), count)]


def scatter_about(stream_key, shape, deviation, bound, split=(), kind=jnp.bfloat16):
    level = block_scale(stream_key, shape, split, -0.22, 0.18) if split else 1.0
    values = jax.random.normal(stream_key, shape, jnp.float32) * deviation * level
    return jnp.minimum(jnp.maximum(values, -bound), bound).astype(kind)


def bell_draw_with(stream_key, dims, deviation, limit, pieces, heavy, kind=jnp.bfloat16):
    drawn = deviation * jax.random.normal(stream_key, dims, jnp.float32)
    if pieces:
        drawn = drawn * block_scale(stream_key, dims, pieces, -0.22, 0.18)
    return jnp.clip(spiked(drawn, jax.random.fold_in(stream_key, 3), *heavy), -limit, limit).astype(kind)


def setup_inputs(seed: int = 0) -> dict:
    arg_keys = jax.random.split(jax.random.key(seed), 8)
    query_rows = draw_query_rows(jax.random.fold_in(arg_keys[7], 71), 0)
    key_rows = draw_key_rows(jax.random.fold_in(arg_keys[7], 71), 0)
    value_rows = scatter_about(arg_keys[2], (SEQS, LEN, HD), 1.0, 6.0, ((0, 16), (1, 16)))
    out_grads = draw_out_grads(jax.random.fold_in(arg_keys[7], 71), 0)
    layer_input = bell_draw_with(arg_keys[4], (SEQS, LEN, D), 1.0, 6.0, ((0, 16), (1, 16)), (1, 2, 16, 2.0))
    doc_ids = jax.vmap(lambda own: jnp.searchsorted(jnp.cumsum(uneven(own, DOCS, LEN, LEN // 2, 2)), jnp.arange(LEN), side="right"))(jax.random.split(arg_keys[5], SEQS)).reshape((SEQS, LEN)).astype(jnp.int32)
    pair_span = jax.random.permutation(arg_keys[6], PAIRS).astype(jnp.int32)
    return dict(query_rows=query_rows, key_rows=key_rows, value_rows=value_rows, out_grads=out_grads, layer_input=layer_input, doc_ids=doc_ids, pair_span=pair_span)


THETA_BASE = 500000.0

def rope_table(seq_len, head_dim):
    inverse_freq = THETA_BASE ** (-2.0 * np.arange(head_dim // 2) / head_dim)
    angles = np.arange(seq_len)[:, None] * inverse_freq[None, :]
    angles = np.concatenate([angles, angles], axis=1)
    return (np.cos(angles).astype(np.float32), np.sin(angles).astype(np.float32))

def stored_positions(pair_span, pairs, span_len):
    block_index = jnp.arange(2 * pairs, dtype=jnp.int32)
    owner_pair = pair_span[block_index // 2]
    span_index = jnp.where(block_index % 2 == 0, owner_pair, 2 * pairs - 1 - owner_pair)
    row_index = jnp.arange(2 * pairs * span_len, dtype=jnp.int32)
    return (span_index[row_index // span_len] * span_len + row_index % span_len, span_index)

def unrotate(grad_rows, cosine, sine_rows):
    half_dim = grad_rows.shape[-1] // 2
    turned = jnp.concatenate([-grad_rows[..., half_dim:], grad_rows[..., :half_dim]], axis=-1)
    return grad_rows * cosine - turned * sine_rows

def sequence_grads(query_rows, key_rows, value_rows, out_grads, seq_docs, positions, cosine, sine_rows):
    score_scale = 1.0 / math.sqrt(HD)
    query_wide = query_rows.reshape(LEN, H, HD).astype(jnp.float32)
    key_wide = key_rows.astype(jnp.float32)
    value_wide = value_rows.astype(jnp.float32)
    grad_wide = out_grads.reshape(LEN, H, HD).astype(jnp.float32)
    row_docs = seq_docs[positions]
    allowed = (positions[None, :] <= positions[:, None]) & (row_docs[None, :] == row_docs[:, None])
    scores = jnp.einsum('ihd,jd->hij', query_wide, key_wide) * score_scale
    masked = jnp.where(allowed[None], scores, -jnp.inf)
    row_top = lax.optimization_barrier(jnp.max(masked, axis=2, keepdims=True))
    weights = jnp.where(allowed[None], jnp.exp(scores - row_top), 0.0)
    prob_rows = weights / lax.optimization_barrier(jnp.sum(weights, axis=2, keepdims=True))
    dprobs = jnp.einsum('ihd,jd->hij', grad_wide, value_wide)
    row_delta = lax.optimization_barrier(jnp.sum(prob_rows * dprobs, axis=2, keepdims=True))
    dscores = prob_rows * (dprobs - row_delta)
    probs_low = lax.optimization_barrier(prob_rows.astype(jnp.bfloat16)).astype(jnp.float32)
    dscores_low = lax.optimization_barrier(dscores.astype(jnp.bfloat16)).astype(jnp.float32)
    grad_v = jnp.einsum('hij,ihd->jd', probs_low, grad_wide)
    grad_q = jnp.einsum('hij,jd->ihd', dscores_low, key_wide) * score_scale
    grad_k = jnp.einsum('hij,ihd->jd', dscores_low, query_wide) * score_scale
    grad_q = unrotate(grad_q, cosine[:, None, :], sine_rows[:, None, :])
    grad_k = unrotate(grad_k, cosine, sine_rows)
    joined = jnp.concatenate([grad_q.reshape(LEN, H * HD), grad_k, grad_v], axis=1).astype(jnp.bfloat16)
    return (joined, jnp.max(jnp.abs(dscores)))

def reference(query_rows, key_rows, value_rows, out_grads, layer_input, doc_ids, pair_span):
    positions, span_index = stored_positions(pair_span, PAIRS, SPAN)
    cos_tab, sin_tab = rope_table(LEN, HD)
    cosine = jnp.asarray(cos_tab)[positions]
    sine_rows = jnp.asarray(sin_tab)[positions]

    def per_sequence(operands):
        query_one, key_one, value_one, grad_one, docs_one = operands
        return sequence_grads(query_one, key_one, value_one, grad_one, docs_one, positions, cosine, sine_rows)
    grad_qkv, ds_maxima = lax.map(per_sequence, (query_rows, key_rows, value_rows, out_grads, doc_ids))
    grad_weight = jnp.dot(layer_input.reshape(SEQS * LEN, D).T, grad_qkv.reshape(SEQS * LEN, QKV), preferred_element_type=jnp.float32)
    out_max = jnp.max(jnp.abs(out_grads)).astype(jnp.float32)
    maxima = jnp.stack([out_max, jnp.max(ds_maxima)])
    amax_record = jnp.broadcast_to(maxima, (SEQS, PAIRS, 2))
    return (grad_qkv, grad_weight, amax_record)
```

```python
import math

import jax
import jax.numpy as jnp
import numpy as np
from jax import lax
from jax.experimental import pallas as pl
from jax.experimental.pallas import tpu as pltpu
from jax.sharding import PartitionSpec as P

MESH = pl.DeviceIdType.MESH
THETA_BASE = 500000.0
LOG2E = 1.4426950408889634
NEG_LARGE = -1e30
HEADS, HEAD_DIM, SPAN, KEY_BLOCK = 8, 128, 96, 256
TOKENS = 2 * SPAN
SIDE, DEPTH = 4, 8
PAIRS = 2 * DEPTH
SEQ = PAIRS * TOKENS
Q_WIDTH = HEADS * HEAD_DIM
WIDTH = Q_WIDTH + 2 * HEAD_DIM
LANES = HEADS * SPAN
F32, BF16 = jnp.float32, jnp.bfloat16


class Place:
    def __init__(self):
        dp, context = lax.axis_index("dp"), lax.axis_index("context")
        self.context = context
        self.y, self.x = dp // SIDE, dp % SIDE
        self.z, self.core = context // 2, context % 2
        z_next, z_prev = (self.z + 1) % DEPTH, (self.z + DEPTH - 1) % DEPTH
        self.z_up, self.z_down = (dp, z_next * 2 + self.core), (dp, z_prev * 2 + self.core)
        self.x_up = (self.y * SIDE + (self.x + 1) % SIDE, context)
        self.x_down = (self.y * SIDE + (self.x + SIDE - 1) % SIDE, context)
        self.y_up = ((self.y + 1) % SIDE * SIDE + self.x, context)
        self.y_down = ((self.y + SIDE - 1) % SIDE * SIDE + self.x, context)
        self.sibling = (dp, context + 1 - 2 * self.core)
        self.rings = ((self.x, self.x_up, self.x_down), (self.y, self.y_up, self.y_down))

    def greet(self):
        barrier = pltpu.get_barrier_semaphore()
        peers = (self.z_up, self.z_down, self.x_up, self.x_down, self.y_up, self.y_down, self.sibling)
        for peer in peers:
            pl.semaphore_signal(barrier, inc=1, device_id=peer, device_id_type=MESH)
        pl.semaphore_wait(barrier, len(peers))


class Copies:
    def __init__(self, send, recv):
        self.send, self.recv, self.all = send, recv, []

    def start(self, src, dst, device):
        i = len(self.all)
        copy = pltpu.make_async_remote_copy(
            src_ref=src, dst_ref=dst, send_sem=self.send.at[i], recv_sem=self.recv.at[i],
            device_id=device, device_id_type=MESH,
        )
        copy.start()
        self.all.append(copy)
        return copy

    def finish(self):
        for copy in self.all:
            copy.wait_send()


FRONT_COPIES = 62


def front_kernel(k_ref, v_ref, x_ref, kv_ref, xa_ref, xb_ref, transit, send, recv, local):
    at = Place()
    at.greet()
    copies = Copies(send, recv)
    planes = (k_ref, v_ref)
    own = [pltpu.make_async_copy(planes[p], kv_ref.at[at.context, p], local.at[p]) for p in range(2)]
    up, down, side = {}, {}, []
    for p in range(2):
        dst = kv_ref.at[at.context, p]
        up[1, p] = copies.start(planes[p], dst, at.z_up)
        down[1, p] = copies.start(planes[p], dst, at.z_down)
    for p in range(2):
        side.append(copies.start(planes[p], kv_ref.at[at.context, p], at.sibling))

    def column(yy, xx, part):
        return pl.ds(pl.multiple_of(((yy * SIDE + xx) * 2 + part) * 256, 256), 256)

    columns_of = (lambda dest, j: column(j, dest, 0), lambda dest, j: column(dest, j, 1))
    outs = (xa_ref, xb_ref)
    far, near = {}, []
    for g, (n, right, left) in enumerate(at.rings):
        dest = (n + 2) % SIDE
        for j in range(2):
            far[g, 0, j] = copies.start(x_ref.at[:, columns_of[g](dest, j)], transit.at[g, 0, j], right)
            far[g, 1, j] = copies.start(x_ref.at[:, columns_of[g](dest, j + 2)], transit.at[g, 1, j], left)
    for g, (n, right, left) in enumerate(at.rings):
        for j in range(SIDE):
            dst = outs[g].at[n, :, j * 256:(j + 1) * 256]
            near.append(copies.start(x_ref.at[:, columns_of[g]((n + 1) % SIDE, j)], dst, right))
            near.append(copies.start(x_ref.at[:, columns_of[g]((n + 3) % SIDE, j)], dst, left))
    for g, (n, right, left) in enumerate(at.rings):
        for j in range(SIDE):
            src = x_ref.at[:, columns_of[g](n, j)]
            own.append(pltpu.make_async_copy(src, outs[g].at[n, :, j * 256:(j + 1) * 256], local.at[len(own)]))
    for copy in own:
        copy.start()

    for t in range(1, 5):
        for p in range(2):
            if (t, p) in up:
                up[t, p].wait_recv()
                block = kv_ref.at[(at.z + DEPTH - t) % DEPTH * 2 + at.core, p]
                if t < 3 or (t == 3 and p == 0):
                    up[t + 1, p] = copies.start(block, block, at.z_up)
                side.append(copies.start(block, block, at.sibling))
            if (t, p) in down:
                down[t, p].wait_recv()
                block = kv_ref.at[(at.z + t) % DEPTH * 2 + at.core, p]
                if t < 3 or (t == 3 and p == 1):
                    down[t + 1, p] = copies.start(block, block, at.z_down)
                side.append(copies.start(block, block, at.sibling))
    for g, (n, right, left) in enumerate(at.rings):
        for j in range(2):
            far[g, 0, j].wait_recv()
            dst = outs[g].at[(n + 3) % SIDE, :, j * 256:(j + 1) * 256]
            near.append(copies.start(transit.at[g, 0, j], dst, right))
            far[g, 1, j].wait_recv()
            dst = outs[g].at[(n + 1) % SIDE, :, (j + 2) * 256:(j + 3) * 256]
            near.append(copies.start(transit.at[g, 1, j], dst, left))
    for copy in side + near:
        copy.wait_recv()
    for copy in own:
        copy.wait()
    copies.finish()


def any_spec():
    return pl.BlockSpec(memory_space=pl.ANY)


def vmem_spec():
    return pl.BlockSpec(memory_space=pltpu.VMEM)


def front(keys, values, inputs):
    half = inputs.shape[1] // 8
    return pl.pallas_call(
        front_kernel,
        out_shape=(
            jax.ShapeDtypeStruct((PAIRS, 2, TOKENS, HEAD_DIM), BF16),
            jax.ShapeDtypeStruct((SIDE, TOKENS, half), BF16),
            jax.ShapeDtypeStruct((SIDE, TOKENS, half), BF16),
        ),
        in_specs=[any_spec()] * 3,
        out_specs=(vmem_spec(),) * 3,
        scratch_shapes=[
            pltpu.VMEM((2, 2, 2, TOKENS, 256), BF16),
            pltpu.SemaphoreType.DMA((FRONT_COPIES,)),
            pltpu.SemaphoreType.DMA((FRONT_COPIES,)),
            pltpu.SemaphoreType.DMA((10,)),
        ],
        compiler_params=pltpu.CompilerParams(collective_id=0, has_side_effects=True, vmem_limit_bytes=12 << 20),
        name="front",
    )(keys, values, inputs)


def trig_tables():
    inverse_freq = THETA_BASE ** (-2.0 * np.arange(HEAD_DIM // 2) / HEAD_DIM)
    freq = np.concatenate([inverse_freq, inverse_freq])
    sign = np.concatenate([np.ones(HEAD_DIM // 2), -np.ones(HEAD_DIM // 2)])
    base = (np.arange(2 * PAIRS) * SPAN)[:, None] * freq[None, :]
    step = np.arange(SPAN)[:, None] * freq[None, :]
    return (
        np.stack([np.cos(base), np.sin(base)]).astype(np.float32),
        np.stack([np.cos(step), np.sin(step)]).astype(np.float32),
        sign.astype(np.float32).reshape(1, HEAD_DIM),
    )


def fold8(x, op):
    out = x[0:8]
    for r in range(8, x.shape[0], 8):
        out = op(out, x[r:r + 8])
    return out


def attention_kernel(
    pair_ref, query_ref, out_ref, kv_ref, docs_ref, row_ref, base_ref, step_ref, sign_ref,
    gq_ref, dkv_ref, trig_ref, top_ref,
    k_pos, v_pos, qs, gs, s_scr, d_scr, dk_acc, dv_acc, dq_acc,
):
    me = lax.axis_index("context")
    scale = 1.0 / math.sqrt(HEAD_DIM)

    def stored_spans():
        for p in range(PAIRS):
            low = pair_ref[p]
            for half, s in ((0, low), (1, 2 * PAIRS - 1 - low)):
                yield p, pl.ds(half * SPAN, SPAN), pl.ds(pl.multiple_of(s * SPAN, 32), SPAN)

    for p, rows, at in stored_spans():
        k_pos[at, :] = kv_ref[p, 0, rows, :]
        v_pos[at, :] = kv_ref[p, 1, rows, :]
    dk_acc[...] = jnp.zeros_like(dk_acc)
    dv_acc[...] = jnp.zeros_like(dv_acc)
    docs_all = docs_ref[:, 0:SPAN]
    starts = [
        jnp.sum(jnp.sum(jnp.where(docs_all < d, 1.0, 0.0), axis=1, keepdims=True), axis=0, keepdims=True)
        for d in range(1, 8)
    ]

    ds_top = jnp.zeros((8, LANES), F32)
    own_low = pair_ref[me]
    for half in range(2):
        s = own_low if half == 0 else 2 * PAIRS - 1 - own_low
        first = half * SPAN
        for h in range(HEADS):
            head = slice(h * HEAD_DIM, (h + 1) * HEAD_DIM)
            qs[h * SPAN:(h + 1) * SPAN, :] = query_ref[first:first + SPAN, head]
            gs[h * SPAN:(h + 1) * SPAN, :] = out_ref[first:first + SPAN, head]
        own_docs = docs_ref[pl.ds(s, 1), :]
        start = jnp.zeros((1, LANES), F32)
        for d in range(1, 8):
            start = jnp.where(own_docs == d, starts[d - 1], start)
        start = start.astype(jnp.int32)
        q_pos = row_ref[...] + s * SPAN
        lo = jnp.min(start) // KEY_BLOCK
        hi = (s * SPAN + SPAN - 1) // KEY_BLOCK + 1
        dq_acc[...] = jnp.zeros_like(dq_acc)

        def block_rows(b):
            return pl.ds(pl.multiple_of(b * KEY_BLOCK, KEY_BLOCK), KEY_BLOCK)

        def score(b, top):
            sc = lax.dot_general(
                k_pos[block_rows(b), :], qs[...], (((1,), (1,)), ((), ())), preferred_element_type=F32
            )
            key_pos = b * KEY_BLOCK + lax.broadcasted_iota(jnp.int32, (KEY_BLOCK, LANES), 0)
            sc = jnp.where((key_pos <= q_pos) & (key_pos >= start), sc, NEG_LARGE)
            s_scr[b] = sc
            return jnp.maximum(top, fold8(sc, jnp.maximum))

        top = lax.fori_loop(lo, hi, score, jnp.full((8, LANES), NEG_LARGE, F32))
        top = jnp.max(top, axis=0, keepdims=True)

        def weigh(b, state):
            total, weighted = state
            dp = lax.dot_general(
                v_pos[block_rows(b), :], gs[...], (((1,), (1,)), ((), ())), preferred_element_type=F32
            )
            e = jnp.exp2((s_scr[b] - top) * (scale * LOG2E))
            s_scr[b] = e
            d_scr[b] = dp
            return total + fold8(e, jnp.add), weighted + fold8(e * dp, jnp.add)

        zero = jnp.zeros((8, LANES), F32)
        total, weighted = lax.fori_loop(lo, hi, weigh, (zero, zero))
        inverse = 1.0 / jnp.sum(total, axis=0, keepdims=True)
        delta = jnp.sum(weighted, axis=0, keepdims=True) * inverse

        def grads(b, high):
            at = block_rows(b)
            p = s_scr[b] * inverse
            ds = p * (d_scr[b] - delta)
            p16, ds16 = p.astype(BF16), ds.astype(BF16)
            dv_acc[at, :] += jnp.dot(p16, gs[...], preferred_element_type=F32)
            dk_acc[at, :] += jnp.dot(ds16, qs[...], preferred_element_type=F32)
            dq_acc[...] += lax.dot_general(
                k_pos[at, :], ds16, (((0,), (0,)), ((), ())), preferred_element_type=F32
            )
            return jnp.maximum(high, fold8(jnp.abs(ds), jnp.maximum))

        ds_top = lax.fori_loop(lo, hi, grads, ds_top)
        cos_a, sin_a = base_ref[0, pl.ds(s, 1), :], base_ref[1, pl.ds(s, 1), :]
        cos_b, sin_b = step_ref[0], step_ref[1]
        cosine = cos_a * cos_b - sin_a * sin_b
        sine = (sin_a * cos_b + cos_a * sin_b) * sign_ref[...]
        trig_ref[0, first:first + SPAN, :] = cosine
        trig_ref[1, first:first + SPAN, :] = sine
        dq = dq_acc[...].T * scale
        for h in range(HEADS):
            v = dq[h * SPAN:(h + 1) * SPAN, :]
            turned = v * cosine + pltpu.roll(v, HEAD_DIM // 2, 1) * sine
            gq_ref[first:first + SPAN, h * HEAD_DIM:(h + 1) * HEAD_DIM] = turned.astype(BF16)

    for p, rows, at in stored_spans():
        dkv_ref[p, 0, rows, :] = dk_acc[at, :].astype(dkv_ref.dtype)
        dkv_ref[p, 1, rows, :] = dv_acc[at, :].astype(dkv_ref.dtype)
    out_top = jnp.max(fold8(jnp.abs(out_ref[...].astype(F32)), jnp.maximum))
    lane = lax.broadcasted_iota(jnp.int32, top_ref.shape, 1)
    top_ref[...] = jnp.where(lane == 0, out_top, jnp.max(ds_top))


def attention(pair_span, query, out, kv, docs):
    docs_wide = jnp.tile(docs.reshape(2 * PAIRS, SPAN), (1, HEADS))
    row = jnp.asarray(np.tile(np.arange(SPAN, dtype=np.int32), HEADS).reshape(1, LANES))
    base, step, sign = (jnp.asarray(t) for t in trig_tables())
    return pl.pallas_call(
        attention_kernel,
        out_shape=(
            jax.ShapeDtypeStruct((TOKENS, Q_WIDTH), BF16),
            jax.ShapeDtypeStruct((PAIRS, 2, TOKENS, HEAD_DIM), BF16),
            jax.ShapeDtypeStruct((2, TOKENS, HEAD_DIM), F32),
            jax.ShapeDtypeStruct((8, 128), F32),
        ),
        in_specs=[pl.BlockSpec(memory_space=pltpu.SMEM)] + [vmem_spec()] * 8,
        out_specs=(vmem_spec(),) * 4,
        scratch_shapes=[
            pltpu.VMEM((SEQ, HEAD_DIM), BF16),
            pltpu.VMEM((SEQ, HEAD_DIM), BF16),
            pltpu.VMEM((LANES, HEAD_DIM), BF16),
            pltpu.VMEM((LANES, HEAD_DIM), BF16),
            pltpu.VMEM((SEQ // KEY_BLOCK, KEY_BLOCK, LANES), F32),
            pltpu.VMEM((SEQ // KEY_BLOCK, KEY_BLOCK, LANES), F32),
            pltpu.VMEM((SEQ, HEAD_DIM), F32),
            pltpu.VMEM((SEQ, HEAD_DIM), F32),
            pltpu.VMEM((HEAD_DIM, LANES), F32),
        ],
        compiler_params=pltpu.CompilerParams(vmem_limit_bytes=40 << 20),
        name="attention",
    )(pair_span, query, out, kv, docs_wide, row, base, step, sign)


MIDDLE_COPIES = 64


def middle_kernel(
    gq_ref, dkv_ref, trig_ref, top_ref, gx_ref, gy_ref, rows_ref, high_ref,
    sib, up_send, up_recv, down_send, down_recv, gkv, tops, top_send, send, recv, local,
):
    at = Place()
    at.greet()
    copies = Copies(send, recv)
    gathered = (gx_ref, gy_ref)
    q_cols, kv_cols = pl.ds(0, Q_WIDTH), pl.ds(Q_WIDTH, 2 * HEAD_DIM)
    halves = (pl.ds(0, Q_WIDTH // 2), pl.ds(Q_WIDTH // 2, Q_WIDTH // 2))
    kv_halves = (pl.ds(Q_WIDTH, HEAD_DIM), pl.ds(Q_WIDTH + HEAD_DIM, HEAD_DIM))

    side_top = copies.start(top_ref, tops.at[0], at.sibling)
    sides = {}
    for shift in (4, 5, 3, 6, 2, 7, 1, 0):
        dest = (at.z + shift) % DEPTH
        sides[shift] = copies.start(dkv_ref.at[dest, 1 - at.core], sib.at[dest], at.sibling)
    from_left, from_right = {}, {}
    for g, (n, right, left) in enumerate(at.rings):
        dst = gathered[g].at[n, :, q_cols]
        from_left[g] = copies.start(gq_ref, dst, right)
        from_right[g] = copies.start(gq_ref, dst, left)
    own = [
        pltpu.make_async_copy(gq_ref, gathered[g].at[n, :, q_cols], local.at[g])
        for g, (n, right, left) in enumerate(at.rings)
    ]
    own.append(pltpu.make_async_copy(gq_ref, rows_ref.at[:, q_cols], local.at[2]))
    for copy in own:
        copy.start()

    def part(dest, p):
        return dkv_ref[dest, at.core, p].astype(F32) + sib[dest, p].astype(F32)

    side_top.wait_recv()
    high = jnp.maximum(top_ref[...], tops[0])
    ups, downs, up_tops, down_tops, waiting = {}, {}, {}, {}, []
    for t in range(1, 5):
        shift_up, shift_down = 5 - t, 3 + t
        for shift in {shift_up, shift_down}:
            sides[shift].wait_recv()
        if t > 1:
            up_tops[t - 1].wait_recv()
            down_tops[t - 1].wait_recv()
            top_send[0, t - 1] = jnp.maximum(high, tops[2 * t - 3])
            top_send[1, t - 1] = jnp.maximum(high, tops[2 * t - 2])
        else:
            top_send[0, 0] = high
            top_send[1, 0] = high
        up_tops[t] = copies.start(top_send.at[0, t - 1], tops.at[2 * t - 1], at.z_up)
        down_tops[t] = copies.start(top_send.at[1, t - 1], tops.at[2 * t], at.z_down)
        for p in range(2):
            for up in (True, False):
                if t == 1 and up != (p == 0):
                    continue
                moves, sent, got = (ups, up_send, up_recv) if up else (downs, down_send, down_recv)
                value = part((at.z + (shift_up if up else shift_down)) % DEPTH, p)
                if (t - 1, p) in moves:
                    moves[t - 1, p].wait_recv()
                    value = value + got[t - 2, p].astype(F32)
                sent[t - 1, p] = value.astype(BF16)
                moves[t, p] = copies.start(sent.at[t - 1, p], got.at[t - 1, p], at.z_up if up else at.z_down)
        if t == 3:
            for g, (n, right, left) in enumerate(at.rings):
                from_left[g].wait_recv()
                block = gathered[g].at[(n + 3) % SIDE, :, halves[0]]
                waiting.append(copies.start(block, block, right))
                from_right[g].wait_recv()
                block = gathered[g].at[(n + 1) % SIDE, :, halves[1]]
                waiting.append(copies.start(block, block, left))
    scale = 1.0 / math.sqrt(HEAD_DIM)
    sides[0].wait_recv()
    sums = []
    for p in range(2):
        ups[4, p].wait_recv()
        downs[4, p].wait_recv()
        sums.append(part(at.z, p) + up_recv[3, p].astype(F32) + down_recv[3, p].astype(F32))
    gk = sums[0] * scale
    gk = gk * trig_ref[0] + pltpu.roll(gk, HEAD_DIM // 2, 1) * trig_ref[1]
    gkv[:, 0:HEAD_DIM] = gk.astype(BF16)
    gkv[:, HEAD_DIM:] = sums[1].astype(BF16)
    from_left, from_right = {}, {}
    for g, (n, right, left) in enumerate(at.rings):
        dst = gathered[g].at[n, :, kv_cols]
        from_left[g] = copies.start(gkv, dst, right)
        from_right[g] = copies.start(gkv, dst, left)
    up_tops[4].wait_recv()
    down_tops[4].wait_recv()
    high = jnp.maximum(jnp.maximum(high, tops[7]), tops[8])
    top_send[0, 4] = high
    x_left = copies.start(top_send.at[0, 4], tops.at[9], at.x_up)
    x_right = copies.start(top_send.at[0, 4], tops.at[10], at.x_down)
    rows_ref[:, kv_cols] = gkv[...]
    for g, (n, right, left) in enumerate(at.rings):
        gathered[g][n, :, kv_cols] = gkv[...]
    for g, (n, right, left) in enumerate(at.rings):
        from_left[g].wait_recv()
        block = gathered[g].at[(n + 3) % SIDE, :, kv_halves[0]]
        waiting.append(copies.start(block, block, right))
        from_right[g].wait_recv()
        block = gathered[g].at[(n + 1) % SIDE, :, kv_halves[1]]
        waiting.append(copies.start(block, block, left))
    x_left.wait_recv()
    x_far = copies.start(tops.at[9], tops.at[11], at.x_up)
    x_right.wait_recv()
    x_far.wait_recv()
    high_ref[...] = jnp.maximum(jnp.maximum(high, tops[9]), jnp.maximum(tops[10], tops[11]))
    for copy in waiting:
        copy.wait_recv()
    for copy in own:
        copy.wait()
    copies.finish()


def middle(gq, dkv, trig, top):
    block = (TOKENS, HEAD_DIM)
    return pl.pallas_call(
        middle_kernel,
        out_shape=(
            jax.ShapeDtypeStruct((SIDE, TOKENS, WIDTH), BF16),
            jax.ShapeDtypeStruct((SIDE, TOKENS, WIDTH), BF16),
            jax.ShapeDtypeStruct((TOKENS, WIDTH), BF16),
            jax.ShapeDtypeStruct((8, 128), F32),
        ),
        in_specs=[vmem_spec()] * 4,
        out_specs=(vmem_spec(),) * 4,
        scratch_shapes=[
            pltpu.VMEM((DEPTH, 2) + block, BF16),
            pltpu.VMEM((4, 2) + block, BF16),
            pltpu.VMEM((4, 2) + block, BF16),
            pltpu.VMEM((4, 2) + block, BF16),
            pltpu.VMEM((4, 2) + block, BF16),
            pltpu.VMEM((TOKENS, 2 * HEAD_DIM), BF16),
            pltpu.VMEM((12, 8, 128), F32),
            pltpu.VMEM((2, 5, 8, 128), F32),
            pltpu.SemaphoreType.DMA((MIDDLE_COPIES,)),
            pltpu.SemaphoreType.DMA((MIDDLE_COPIES,)),
            pltpu.SemaphoreType.DMA((3,)),
        ],
        compiler_params=pltpu.CompilerParams(collective_id=1, has_side_effects=True, vmem_limit_bytes=16 << 20),
        name="middle",
    )(gq, dkv, trig, top)


FINISH_COPIES = 32
SLICE = 32


def finish_kernel(
    pa_ref, pb_ref, top_ref, w_ref, high_ref,
    sib, far_send, far_recv, near_send, near_recv, total, up_send, up_recv, down_send, down_recv, tops,
    send, recv,
):
    at = Place()
    at.greet()
    copies = Copies(send, recv)
    partial = (pa_ref, pb_ref)
    sides = {}
    for hop in (2, 1, 3, 0):
        for g, (n, right, left) in enumerate(at.rings):
            dest = (n + hop) % SIDE
            dest = (at.rings[1 - g][0] + hop) % SIDE
            sides[g, hop] = copies.start(partial[g].at[dest, :, 1 - at.core], sib.at[g, dest], at.sibling)
    y_left = copies.start(top_ref, tops.at[0], at.y_up)
    y_right = copies.start(top_ref, tops.at[1], at.y_down)

    def part(g, dest, rows):
        return partial[g][dest, rows, at.core].astype(F32) + sib[g, dest, rows].astype(F32)

    low, high_half = slice(0, 2), slice(2, 4)
    fars, nears = {}, {}
    for g in range(2):
        n, right, left = at.rings[1 - g]
        dest = (n + 2) % SIDE
        sides[g, 2].wait_recv()
        far_send[g, 0] = part(g, dest, low).astype(BF16)
        fars[g, 0] = copies.start(far_send.at[g, 0], far_recv.at[g, 0], right)
        far_send[g, 1] = part(g, dest, high_half).astype(BF16)
        fars[g, 1] = copies.start(far_send.at[g, 1], far_recv.at[g, 1], left)
    for g in range(2):
        n, right, left = at.rings[1 - g]
        sides[g, 1].wait_recv()
        dest = (n + 1) % SIDE
        near_send[g, 0, 2:4] = part(g, dest, high_half).astype(BF16)
        fars[g, 0].wait_recv()
        near_send[g, 0, 0:2] = (part(g, dest, low) + far_recv[g, 0].astype(F32)).astype(BF16)
        nears[g, 0] = copies.start(near_send.at[g, 0], near_recv.at[g, 0], right)
        sides[g, 3].wait_recv()
        dest = (n + 3) % SIDE
        near_send[g, 1, 0:2] = part(g, dest, low).astype(BF16)
        fars[g, 1].wait_recv()
        near_send[g, 1, 2:4] = (part(g, dest, high_half) + far_recv[g, 1].astype(F32)).astype(BF16)
        nears[g, 1] = copies.start(near_send.at[g, 1], near_recv.at[g, 1], left)
    y_left.wait_recv()
    y_far = copies.start(tops.at[0], tops.at[2], at.y_up)
    for g in range(2):
        n, right, left = at.rings[1 - g]
        sides[g, 0].wait_recv()
        nears[g, 0].wait_recv()
        nears[g, 1].wait_recv()
        total[4 * g:4 * g + 4] = (
            part(g, n, slice(0, 4)) + near_recv[g, 0].astype(F32) + near_recv[g, 1].astype(F32)
        )
    y_right.wait_recv()
    y_far.wait_recv()
    high_ref[...] = jnp.maximum(jnp.maximum(top_ref[...], tops[0]), jnp.maximum(tops[1], tops[2]))

    middle_col = w_ref.shape[1] // 2
    first, second = slice(0, middle_col), slice(middle_col, 2 * middle_col)
    ups, downs = {}, {}
    dest = (at.z + 4) % DEPTH
    up_send[0] = total[dest].astype(BF16)
    ups[1] = copies.start(up_send.at[0, :, pl.ds(0, middle_col)], up_recv.at[0, :, pl.ds(0, middle_col)], at.z_up)
    downs[1] = copies.start(
        up_send.at[0, :, pl.ds(middle_col, middle_col)],
        down_recv.at[0, :, pl.ds(middle_col, middle_col)],
        at.z_down,
    )
    for t in range(2, 5):
        for up in (True, False):
            moves, sent, got, device = (
                (ups, up_send, up_recv, at.z_up) if up else (downs, down_send, down_recv, at.z_down)
            )
            dest = (at.z + (5 - t if up else 3 + t)) % DEPTH
            if t == 2:
                joined, alone = (first, second) if up else (second, first)
                sent[1, :, alone] = total[dest, :, alone].astype(BF16)
                moves[1].wait_recv()
                sent[1, :, joined] = (total[dest, :, joined] + got[0, :, joined].astype(F32)).astype(BF16)
            else:
                moves[t - 1].wait_recv()
                sent[t - 1] = (total[dest] + got[t - 2].astype(F32)).astype(BF16)
            moves[t] = copies.start(sent.at[t - 1], got.at[t - 1], device)
    ups[4].wait_recv()
    downs[4].wait_recv()
    w_ref[...] = total[at.z] + up_recv[3].astype(F32) + down_recv[3].astype(F32)
    copies.finish()


def finish(pa, pb, top):
    quarter = (DEPTH // 2, SLICE, WIDTH)
    return pl.pallas_call(
        finish_kernel,
        out_shape=(jax.ShapeDtypeStruct((SLICE, WIDTH), F32), jax.ShapeDtypeStruct((8, 128), F32)),
        in_specs=[vmem_spec()] * 3,
        out_specs=(vmem_spec(),) * 2,
        scratch_shapes=[
            pltpu.VMEM((2, SIDE) + quarter, BF16),
            pltpu.VMEM((2, 2, 2, SLICE, WIDTH), BF16),
            pltpu.VMEM((2, 2, 2, SLICE, WIDTH), BF16),
            pltpu.VMEM((2, 2) + quarter, BF16),
            pltpu.VMEM((2, 2) + quarter, BF16),
            pltpu.VMEM((DEPTH, SLICE, WIDTH), F32),
            pltpu.VMEM((4, SLICE, WIDTH), BF16),
            pltpu.VMEM((4, SLICE, WIDTH), BF16),
            pltpu.VMEM((4, SLICE, WIDTH), BF16),
            pltpu.VMEM((4, SLICE, WIDTH), BF16),
            pltpu.VMEM((3, 8, 128), F32),
            pltpu.SemaphoreType.DMA((FINISH_COPIES,)),
            pltpu.SemaphoreType.DMA((FINISH_COPIES,)),
        ],
        compiler_params=pltpu.CompilerParams(collective_id=2, has_side_effects=True, vmem_limit_bytes=24 << 20),
        name="finish",
    )(pa, pb, top)


def weight_partial(columns, rows):
    half = columns.shape[2]
    partial = lax.dot_general(
        columns.reshape(SIDE * TOKENS, half),
        rows.reshape(SIDE * TOKENS, WIDTH),
        (((0,), (0,)), ((), ())),
        preferred_element_type=F32,
    )
    return partial.astype(BF16).reshape(SIDE, DEPTH // 2, 2, SLICE, WIDTH)


def local(query_rows, key_rows, value_rows, out_grads, layer_input, doc_ids, pair_span):
    kv, xa, xb = front(key_rows[0], value_rows[0], layer_input[0])
    gq, dkv, trig, top = attention(pair_span, query_rows[0], out_grads[0], kv, doc_ids[0])
    gx, gy, rows, top = middle(gq, dkv.reshape(DEPTH, 2, 2, TOKENS, HEAD_DIM), trig, top)
    weight, top = finish(weight_partial(xa, gx), weight_partial(xb, gy), top)
    return rows[None], weight, top[0:1, 0:2].reshape(1, 1, 2)


def solution(mesh):
    in_specs = (
        P("dp", "context", None),
        P("dp", "context", None),
        P("dp", "context", None),
        P("dp", "context", None),
        P("dp", "context", None),
        P("dp", None),
        P(),
    )
    out_specs = (P("dp", "context", None), P(("dp", "context"), None), P("dp", "context", None))
    return jax.shard_map(local, mesh=mesh, in_specs=in_specs, out_specs=out_specs, check_vma=False)
```

```python
import math

import jax
import jax.numpy as jnp
import numpy as np
from jax import lax
from jax.experimental import pallas as pl
from jax.experimental.pallas import tpu as pltpu
from jax.sharding import PartitionSpec as P

MESH = pl.DeviceIdType.MESH
THETA_BASE = 500000.0
LOG2E = 1.4426950408889634
NEG_LARGE = -1e30
HEADS, HEAD_DIM, SPAN, KEY_BLOCK = 8, 128, 96, 256
TOKENS = 2 * SPAN
SIDE, DEPTH = 4, 8
PAIRS = 2 * DEPTH
SEQ = PAIRS * TOKENS
Q_WIDTH = HEADS * HEAD_DIM
WIDTH = Q_WIDTH + 2 * HEAD_DIM
LANES = HEADS * SPAN
F32, BF16 = jnp.float32, jnp.bfloat16
W_TYPE = BF16


class Place:
    def __init__(self):
        dp, context = lax.axis_index("dp"), lax.axis_index("context")
        self.context = context
        self.y, self.x = dp // SIDE, dp % SIDE
        self.z, self.core = context // 2, context % 2
        z_next, z_prev = (self.z + 1) % DEPTH, (self.z + DEPTH - 1) % DEPTH
        self.z_up, self.z_down = (dp, z_next * 2 + self.core), (dp, z_prev * 2 + self.core)
        self.x_up = (self.y * SIDE + (self.x + 1) % SIDE, context)
        self.x_down = (self.y * SIDE + (self.x + SIDE - 1) % SIDE, context)
        self.y_up = ((self.y + 1) % SIDE * SIDE + self.x, context)
        self.y_down = ((self.y + SIDE - 1) % SIDE * SIDE + self.x, context)
        self.sibling = (dp, context + 1 - 2 * self.core)
        self.rings = ((self.x, self.x_up, self.x_down), (self.y, self.y_up, self.y_down))

    def greet(self):
        barrier = pltpu.get_barrier_semaphore()
        peers = (self.z_up, self.z_down, self.x_up, self.x_down, self.y_up, self.y_down, self.sibling)
        for peer in peers:
            pl.semaphore_signal(barrier, inc=1, device_id=peer, device_id_type=MESH)
        pl.semaphore_wait(barrier, len(peers))


class Copies:
    def __init__(self, send, recv):
        self.send, self.recv, self.all = send, recv, []

    def start(self, src, dst, device):
        i = len(self.all)
        copy = pltpu.make_async_remote_copy(
            src_ref=src, dst_ref=dst, send_sem=self.send.at[i], recv_sem=self.recv.at[i],
            device_id=device, device_id_type=MESH,
        )
        copy.start()
        self.all.append(copy)
        return copy

    def finish(self):
        for copy in self.all:
            copy.wait_send()


FRONT_COPIES = 62


def front_kernel(k_ref, v_ref, x_ref, *refs):
    staged, (kv_ref, xa_ref, xb_ref), held, (transit, send, recv, local) = refs[:4], refs[4:7], refs[7:11], refs[11:]
    at = Place()
    at.greet()
    copies = Copies(send, recv)
    planes = (k_ref, v_ref)
    own = [pltpu.make_async_copy(planes[p], kv_ref.at[at.context, p], local.at[p]) for p in range(2)]
    up, down, side = {}, {}, []
    for p in range(2):
        dst = kv_ref.at[at.context, p]
        up[1, p] = copies.start(planes[p], dst, at.z_up)
        down[1, p] = copies.start(planes[p], dst, at.z_down)
    for p in range(2):
        side.append(copies.start(planes[p], kv_ref.at[at.context, p], at.sibling))

    def column(yy, xx, part):
        return pl.ds(pl.multiple_of(((yy * SIDE + xx) * 2 + part) * 256, 256), 256)

    columns_of = (lambda dest, j: column(j, dest, 0), lambda dest, j: column(dest, j, 1))
    outs = (xa_ref, xb_ref)
    far, near = {}, []
    for g, (n, right, left) in enumerate(at.rings):
        dest = (n + 2) % SIDE
        for j in range(2):
            far[g, 0, j] = copies.start(x_ref.at[:, columns_of[g](dest, j)], transit.at[g, 0, j], right)
            far[g, 1, j] = copies.start(x_ref.at[:, columns_of[g](dest, j + 2)], transit.at[g, 1, j], left)
    for g, (n, right, left) in enumerate(at.rings):
        for j in range(SIDE):
            dst = outs[g].at[n, :, j * 256:(j + 1) * 256]
            near.append(copies.start(x_ref.at[:, columns_of[g]((n + 1) % SIDE, j)], dst, right))
            near.append(copies.start(x_ref.at[:, columns_of[g]((n + 3) % SIDE, j)], dst, left))
    for g, (n, right, left) in enumerate(at.rings):
        for j in range(SIDE):
            src = x_ref.at[:, columns_of[g](n, j)]
            own.append(pltpu.make_async_copy(src, outs[g].at[n, :, j * 256:(j + 1) * 256], local.at[len(own)]))
    def relay_inputs():
        for g, (n, right, left) in enumerate(at.rings):
            for j in range(2):
                far[g, 0, j].wait_recv()
                dst = outs[g].at[(n + 3) % SIDE, :, j * 256:(j + 1) * 256]
                near.append(copies.start(transit.at[g, 0, j], dst, right))
                far[g, 1, j].wait_recv()
                dst = outs[g].at[(n + 1) % SIDE, :, (j + 2) * 256:(j + 3) * 256]
                near.append(copies.start(transit.at[g, 1, j], dst, left))

    for src, dst in zip(staged, held):
        own.append(pltpu.make_async_copy(src, dst, local.at[len(own)]))
    for copy in own:
        copy.start()

    for t in range(1, 5):
        if t == 3:
            relay_inputs()
        for p in range(2):
            if (t, p) in up:
                up[t, p].wait_recv()
                block = kv_ref.at[(at.z + DEPTH - t) % DEPTH * 2 + at.core, p]
                if t < 3 or (t == 3 and p == 0):
                    up[t + 1, p] = copies.start(block, block, at.z_up)
                side.append(copies.start(block, block, at.sibling))
            if (t, p) in down:
                down[t, p].wait_recv()
                block = kv_ref.at[(at.z + t) % DEPTH * 2 + at.core, p]
                if t < 3 or (t == 3 and p == 1):
                    down[t + 1, p] = copies.start(block, block, at.z_down)
                side.append(copies.start(block, block, at.sibling))
    for copy in side + near:
        copy.wait_recv()
    for copy in own:
        copy.wait()
    copies.finish()


def hbm_spec():
    return pl.BlockSpec(memory_space=pltpu.HBM)


def vmem_spec():
    return pl.BlockSpec(memory_space=pltpu.VMEM)


def front(keys, values, inputs, *staged):
    half = inputs.shape[1] // 8
    return pl.pallas_call(
        front_kernel,
        out_shape=(
            jax.ShapeDtypeStruct((PAIRS, 2, TOKENS, HEAD_DIM), BF16),
            jax.ShapeDtypeStruct((SIDE, TOKENS, half), BF16),
            jax.ShapeDtypeStruct((SIDE, TOKENS, half), BF16),
        ) + tuple(jax.ShapeDtypeStruct(a.shape, a.dtype) for a in staged),
        in_specs=[hbm_spec()] * 7,
        out_specs=(vmem_spec(),) * 7,
        scratch_shapes=[
            pltpu.VMEM((2, 2, 2, TOKENS, 256), BF16),
            pltpu.SemaphoreType.DMA((FRONT_COPIES,)),
            pltpu.SemaphoreType.DMA((FRONT_COPIES,)),
            pltpu.SemaphoreType.DMA((14,)),
        ],
        compiler_params=pltpu.CompilerParams(collective_id=0, has_side_effects=True, vmem_limit_bytes=12 << 20),
        name="front",
    )(*(pltpu.with_memory_space_constraint(a, pltpu.HBM) for a in (keys, values, inputs) + staged))


def trig_table():
    inverse_freq = THETA_BASE ** (-2.0 * np.arange(HEAD_DIM // 2) / HEAD_DIM)
    freq = np.concatenate([inverse_freq, inverse_freq])
    sign = np.concatenate([np.ones(HEAD_DIM // 2), -np.ones(HEAD_DIM // 2)])
    base = (np.arange(2 * PAIRS) * SPAN)[:, None] * freq[None, :]
    step = np.arange(SPAN)[:, None] * freq[None, :]
    parts = [np.cos(base), np.sin(base) * sign, np.cos(step), np.sin(step) * sign]
    return np.concatenate(parts).astype(np.float32)


def fold8(x, op):
    out = x[0:8]
    for r in range(8, x.shape[0], 8):
        out = op(out, x[r:r + 8])
    return out


def attention_kernel(
    pair_ref, query_ref, out_ref, kv_ref, docs_ref, table_ref,
    gq_ref, dkv_ref, trig_ref, top_ref,
    k_pos, v_pos, qs, gs, s_scr, d_scr, dk_acc, dv_acc, dq_acc,
):
    me = lax.axis_index("context")
    scale = 1.0 / math.sqrt(HEAD_DIM)

    def stored_spans():
        for p in range(PAIRS):
            low = pair_ref[p]
            for half, s in ((0, low), (1, 2 * PAIRS - 1 - low)):
                yield p, pl.ds(half * SPAN, SPAN), pl.ds(pl.multiple_of(s * SPAN, 32), SPAN)

    for p, rows, at in stored_spans():
        k_pos[at, :] = kv_ref[p, 0, rows, :]
        v_pos[at, :] = kv_ref[p, 1, rows, :]
    dk_acc[...] = jnp.zeros_like(dk_acc)
    dv_acc[...] = jnp.zeros_like(dv_acc)
    docs = docs_ref[...]
    starts = [
        jnp.sum(jnp.where(docs < d, 1.0, 0.0), axis=1, keepdims=True).astype(jnp.int32) for d in range(1, 8)
    ]
    lane = lax.broadcasted_iota(jnp.int32, (1, LANES), 1)
    row = lane - SPAN * ((lane * 683) >> 16)

    ds_top = jnp.zeros((8, LANES), F32)
    own_low = pair_ref[me]
    for half in range(2):
        s = own_low if half == 0 else 2 * PAIRS - 1 - own_low
        first = half * SPAN
        for h in range(HEADS):
            head = slice(h * HEAD_DIM, (h + 1) * HEAD_DIM)
            qs[h * SPAN:(h + 1) * SPAN, :] = query_ref[first:first + SPAN, head]
            gs[h * SPAN:(h + 1) * SPAN, :] = out_ref[first:first + SPAN, head]
        q_pos = row + s * SPAN
        start = jnp.zeros((1, LANES), jnp.int32)
        for first_of in starts:
            start = jnp.where(first_of <= q_pos, jnp.maximum(start, first_of), start)
        lo = jnp.min(start) // KEY_BLOCK
        hi = (s * SPAN + SPAN - 1) // KEY_BLOCK + 1
        dq_acc[...] = jnp.zeros_like(dq_acc)

        def block_rows(b):
            return pl.ds(pl.multiple_of(b * KEY_BLOCK, KEY_BLOCK), KEY_BLOCK)

        def score(b, top):
            sc = lax.dot_general(
                k_pos[block_rows(b), :], qs[...], (((1,), (1,)), ((), ())), preferred_element_type=F32
            )
            key_pos = b * KEY_BLOCK + lax.broadcasted_iota(jnp.int32, (KEY_BLOCK, LANES), 0)
            sc = jnp.where((key_pos <= q_pos) & (key_pos >= start), sc, NEG_LARGE)
            s_scr[b] = sc
            return jnp.maximum(top, fold8(sc, jnp.maximum))

        top = lax.fori_loop(lo, hi, score, jnp.full((8, LANES), NEG_LARGE, F32))
        top = jnp.max(top, axis=0, keepdims=True)

        def weigh(b, state):
            total, weighted = state
            dp = lax.dot_general(
                v_pos[block_rows(b), :], gs[...], (((1,), (1,)), ((), ())), preferred_element_type=F32
            )
            e = jnp.exp2((s_scr[b] - top) * (scale * LOG2E))
            s_scr[b] = e
            d_scr[b] = dp
            return total + fold8(e, jnp.add), weighted + fold8(e * dp, jnp.add)

        zero = jnp.zeros((8, LANES), F32)
        total, weighted = lax.fori_loop(lo, hi, weigh, (zero, zero))
        inverse = 1.0 / jnp.sum(total, axis=0, keepdims=True)
        delta = jnp.sum(weighted, axis=0, keepdims=True) * inverse

        def grads(b, high):
            at = block_rows(b)
            p = s_scr[b] * inverse
            ds = p * (d_scr[b] - delta)
            p16, ds16 = p.astype(BF16), ds.astype(BF16)
            dv_acc[at, :] += jnp.dot(p16, gs[...], preferred_element_type=F32)
            dk_acc[at, :] += jnp.dot(ds16, qs[...], preferred_element_type=F32)
            dq_acc[...] += lax.dot_general(
                k_pos[at, :], ds16, (((0,), (0,)), ((), ())), preferred_element_type=F32
            )
            return jnp.maximum(high, fold8(jnp.abs(ds), jnp.maximum))

        ds_top = lax.fori_loop(lo, hi, grads, ds_top)
        cos_a, sin_a = table_ref[pl.ds(s, 1), :], table_ref[pl.ds(2 * PAIRS + s, 1), :]
        cos_b, sin_b = table_ref[4 * PAIRS:4 * PAIRS + SPAN, :], table_ref[4 * PAIRS + SPAN:, :]
        cosine = cos_a * cos_b - sin_a * sin_b
        sine = sin_a * cos_b + cos_a * sin_b
        trig_ref[0, first:first + SPAN, :] = cosine
        trig_ref[1, first:first + SPAN, :] = sine
        dq = dq_acc[...].T * scale
        for h in range(HEADS):
            v = dq[h * SPAN:(h + 1) * SPAN, :]
            turned = v * cosine + pltpu.roll(v, HEAD_DIM // 2, 1) * sine
            gq_ref[first:first + SPAN, h * HEAD_DIM:(h + 1) * HEAD_DIM] = turned.astype(BF16)

    for p, rows, at in stored_spans():
        dkv_ref[p, 0, rows, :] = dk_acc[at, :].astype(dkv_ref.dtype)
        dkv_ref[p, 1, rows, :] = dv_acc[at, :].astype(dkv_ref.dtype)
    out_top = jnp.max(fold8(jnp.abs(out_ref[...].astype(F32)), jnp.maximum))
    column = lax.broadcasted_iota(jnp.int32, top_ref.shape, 1)
    top_ref[...] = jnp.where(column == 0, out_top, jnp.max(ds_top))


def attention(pair_span, query, out, kv, docs, table):
    return pl.pallas_call(
        attention_kernel,
        out_shape=(
            jax.ShapeDtypeStruct((TOKENS, Q_WIDTH), BF16),
            jax.ShapeDtypeStruct((PAIRS, 2, TOKENS, HEAD_DIM), BF16),
            jax.ShapeDtypeStruct((2, TOKENS, HEAD_DIM), F32),
            jax.ShapeDtypeStruct((8, 128), F32),
        ),
        in_specs=[pl.BlockSpec(memory_space=pltpu.SMEM)] + [vmem_spec()] * 5,
        out_specs=(vmem_spec(),) * 4,
        scratch_shapes=[
            pltpu.VMEM((SEQ, HEAD_DIM), BF16),
            pltpu.VMEM((SEQ, HEAD_DIM), BF16),
            pltpu.VMEM((LANES, HEAD_DIM), BF16),
            pltpu.VMEM((LANES, HEAD_DIM), BF16),
            pltpu.VMEM((SEQ // KEY_BLOCK, KEY_BLOCK, LANES), F32),
            pltpu.VMEM((SEQ // KEY_BLOCK, KEY_BLOCK, LANES), F32),
            pltpu.VMEM((SEQ, HEAD_DIM), F32),
            pltpu.VMEM((SEQ, HEAD_DIM), F32),
            pltpu.VMEM((HEAD_DIM, LANES), F32),
        ],
        compiler_params=pltpu.CompilerParams(vmem_limit_bytes=40 << 20),
        name="attention",
    )(pair_span, query, out, kv, docs, table)


TAIL_COPIES = 140
SLICE = 32
CHUNKS = ((0, 512), (512, 512), (1024, 256))


def tail_kernel(
    gq_ref, dkv_ref, trig_ref, top_ref, xa_ref, xb_ref, rows_ref, w_ref, high_ref,
    gx, gy, turned, sib, up_send, up_recv, down_send, down_recv, gkv, tops, top_send,
    partial, partial_sib, far_send, far_recv, near_send, near_recv, total,
    w_up_send, w_up_recv, w_down_send, w_down_recv, send, recv, local,
):
    at = Place()
    at.greet()
    copies = Copies(send, recv)
    gathered, inputs = (gx, gy), (xa_ref, xb_ref)
    q_cols = pl.ds(0, Q_WIDTH)

    from_left, from_right, spreading = {}, {}, {c: [] for c in range(len(CHUNKS))}

    def spread(c):
        first, width = CHUNKS[c]
        src = gkv if first == Q_WIDTH else gq_ref.at[:, pl.ds(first, width)]
        for g, (n, right, left) in enumerate(at.rings):
            dst = gathered[g].at[n, :, pl.ds(first, width)]
            from_left[g, c] = copies.start(src, dst, right)
            from_right[g, c] = copies.start(src, dst, left)

    def relay(c):
        first, width = CHUNKS[c]
        for g, (n, right, left) in enumerate(at.rings):
            from_left[g, c].wait_recv()
            block = gathered[g].at[(n + 3) % SIDE, :, pl.ds(first, width // 2)]
            spreading[c].append(copies.start(block, block, right))
            from_right[g, c].wait_recv()
            block = gathered[g].at[(n + 1) % SIDE, :, pl.ds(first + width // 2, width // 2)]
            spreading[c].append(copies.start(block, block, left))

    sides = {}

    def part(dest, p):
        return dkv_ref[dest, at.core, p].astype(F32) + sib[dest, p].astype(F32)

    ups, downs, up_tops, down_tops = {}, {}, {}, {}

    def key_value_hop(t, high):
        shift_up, shift_down = 5 - t, 3 + t
        for shift in sorted({shift_up, shift_down}):
            sides[shift].wait_recv()
        for p in range(2):
            for up in (True, False):
                if t == 1 and up != (p == 0):
                    continue
                moves, sent, got = (ups, up_send, up_recv) if up else (downs, down_send, down_recv)
                value = part((at.z + (shift_up if up else shift_down)) % DEPTH, p)
                if (t - 1, p) in moves:
                    moves[t - 1, p].wait_recv()
                    value = value + got[t - 2, p].astype(F32)
                sent[t - 1, p] = value.astype(BF16)
                moves[t, p] = copies.start(sent.at[t - 1, p], got.at[t - 1, p], at.z_up if up else at.z_down)
        if t > 1:
            up_tops[t - 1].wait_recv()
            down_tops[t - 1].wait_recv()
            top_send[0, t - 1] = jnp.maximum(high, tops[2 * t - 3])
            top_send[1, t - 1] = jnp.maximum(high, tops[2 * t - 2])
        else:
            top_send[0, 0] = high
            top_send[1, 0] = high
        up_tops[t] = copies.start(top_send.at[0, t - 1], tops.at[2 * t - 1], at.z_up)
        down_tops[t] = copies.start(top_send.at[1, t - 1], tops.at[2 * t], at.z_down)

    crossing, fars, nears, w_ups, w_downs = {}, {}, {}, {}, {}
    ring = (at.rings[1], at.rings[0])
    low, upper = slice(0, 2), slice(2, 4)

    def turn(g):
        for j in range(SIDE):
            block = inputs[g][:, :, j * 256:(j + 1) * 256].reshape(SIDE * TOKENS, 256)
            turned[g, j] = block.T

    def multiply(c):
        first, width = CHUNKS[c]
        cols = pl.ds(first, width)
        for copy in spreading[c]:
            copy.wait_recv()
        for hop in (2, 1, 3, 0):
            for g in range(2):
                dest = (ring[g][0] + hop) % SIDE
                rows = gathered[g][:, :, cols].reshape(SIDE * TOKENS, width)
                product = jnp.dot(turned[g, dest], rows, preferred_element_type=F32)
                partial[g, dest, :, :, :, cols] = product.astype(BF16).reshape(DEPTH // 2, 2, SLICE, width)
                crossing[g, hop, c] = copies.start(
                    partial.at[g, dest, :, 1 - at.core, :, cols], partial_sib.at[g, dest, :, :, cols], at.sibling
                )

    def w_part(g, dest, rows, cols):
        return partial[g, dest, rows, at.core, :, cols].astype(F32) + partial_sib[g, dest, rows, :, cols].astype(F32)

    def far(c):
        cols = pl.ds(*CHUNKS[c])
        for g in range(2):
            n, right, left = ring[g]
            dest = (n + 2) % SIDE
            crossing[g, 2, c].wait_recv()
            for arm, rows, device in ((0, low, right), (1, upper, left)):
                far_send[g, arm, :, :, cols] = w_part(g, dest, rows, cols).astype(BF16)
                fars[g, arm, c] = copies.start(
                    far_send.at[g, arm, :, :, cols], far_recv.at[g, arm, :, :, cols], device
                )

    def near(c):
        cols = pl.ds(*CHUNKS[c])
        for g in range(2):
            n, right, left = ring[g]
            for arm, hop, device in ((0, 1, right), (1, 3, left)):
                dest = (n + hop) % SIDE
                crossing[g, hop, c].wait_recv()
                joined, alone = (low, upper) if arm == 0 else (upper, low)
                near_send[g, arm, alone, :, cols] = w_part(g, dest, alone, cols).astype(BF16)
                fars[g, arm, c].wait_recv()
                value = w_part(g, dest, joined, cols) + far_recv[g, arm, :, :, cols].astype(F32)
                near_send[g, arm, joined, :, cols] = value.astype(BF16)
                nears[g, arm, c] = copies.start(
                    near_send.at[g, arm, :, :, cols], near_recv.at[g, arm, :, :, cols], device
                )

    def gather_total(c):
        cols = pl.ds(*CHUNKS[c])
        for g in range(2):
            crossing[g, 0, c].wait_recv()
            value = w_part(g, ring[g][0], slice(0, 4), cols)
            for arm in range(2):
                nears[g, arm, c].wait_recv()
                value = value + near_recv[g, arm, :, :, cols].astype(F32)
            total[4 * g:4 * g + 4, :, cols] = value

    def w_hop(t, c):
        first, width = CHUNKS[c]
        cols, half = pl.ds(first, width), width // 2
        sides_of = (pl.ds(first, half), pl.ds(first + half, half))
        for up in (True, False):
            moves, sent, got, device = (
                (w_ups, w_up_send, w_up_recv, at.z_up) if up else (w_downs, w_down_send, w_down_recv, at.z_down)
            )
            dest = (at.z + (5 - t if up else 3 + t)) % DEPTH
            joined, alone = sides_of if up else sides_of[::-1]
            if t == 1:
                sent[0, :, joined] = total[dest, :, joined].astype(W_TYPE)
                moves[1, c] = copies.start(sent.at[0, :, joined], got.at[0, :, joined], device)
                continue
            if t == 2:
                sent[1, :, alone] = total[dest, :, alone].astype(W_TYPE)
                moves[1, c].wait_recv()
                sent[1, :, joined] = (total[dest, :, joined] + got[0, :, joined].astype(F32)).astype(W_TYPE)
            else:
                moves[t - 1, c].wait_recv()
                sent[t - 1, :, cols] = (total[dest, :, cols] + got[t - 2, :, cols].astype(F32)).astype(W_TYPE)
            moves[t, c] = copies.start(sent.at[t - 1, :, cols], got.at[t - 1, :, cols], device)

    def w_end(c):
        cols = pl.ds(*CHUNKS[c])
        w_ups[4, c].wait_recv()
        w_downs[4, c].wait_recv()
        w_ref[:, cols] = total[at.z, :, cols] + w_up_recv[3, :, cols].astype(F32) + w_down_recv[3, :, cols].astype(F32)

    spread(0)
    side_top = copies.start(top_ref, tops.at[0], at.sibling)
    for shift in (4, 5, 3, 6, 2, 7, 1, 0):
        dest = (at.z + shift) % DEPTH
        sides[shift] = copies.start(dkv_ref.at[dest, 1 - at.core], sib.at[dest], at.sibling)
    own = [
        pltpu.make_async_copy(gq_ref, gathered[g].at[n, :, q_cols], local.at[g])
        for g, (n, right, left) in enumerate(at.rings)
    ]
    own.append(pltpu.make_async_copy(gq_ref, rows_ref.at[:, q_cols], local.at[2]))
    for copy in own:
        copy.start()
    side_top.wait_recv()
    high = jnp.maximum(top_ref[...], tops[0])
    key_value_hop(1, high)
    spread(1)
    turn(0)
    key_value_hop(2, high)
    turn(1)
    relay(0)
    key_value_hop(3, high)
    relay(1)
    key_value_hop(4, high)
    for copy in own[0:2]:
        copy.wait()
    multiply(0)

    scale = 1.0 / math.sqrt(HEAD_DIM)
    sides[0].wait_recv()
    sums = []
    for p in range(2):
        ups[4, p].wait_recv()
        downs[4, p].wait_recv()
        sums.append(part(at.z, p) + up_recv[3, p].astype(F32) + down_recv[3, p].astype(F32))
    gk = sums[0] * scale
    gk = gk * trig_ref[0] + pltpu.roll(gk, HEAD_DIM // 2, 1) * trig_ref[1]
    gkv[:, 0:HEAD_DIM] = gk.astype(BF16)
    gkv[:, HEAD_DIM:] = sums[1].astype(BF16)
    spread(2)
    rows_ref[:, Q_WIDTH:] = gkv[...]
    for g, (n, right, left) in enumerate(at.rings):
        gathered[g][n, :, Q_WIDTH:] = gkv[...]
    up_tops[4].wait_recv()
    down_tops[4].wait_recv()
    high = jnp.maximum(jnp.maximum(high, tops[7]), tops[8])
    top_send[0, 4] = high
    x_left = copies.start(top_send.at[0, 4], tops.at[9], at.x_up)
    x_right = copies.start(top_send.at[0, 4], tops.at[10], at.x_down)
    far(0)
    multiply(1)
    relay(2)
    x_left.wait_recv()
    x_far = copies.start(tops.at[9], tops.at[11], at.x_up)
    near(0)
    far(1)
    multiply(2)
    x_right.wait_recv()
    x_far.wait_recv()
    high = jnp.maximum(jnp.maximum(high, tops[9]), jnp.maximum(tops[10], tops[11]))
    top_send[1, 4] = high
    y_left = copies.start(top_send.at[1, 4], tops.at[12], at.y_up)
    y_right = copies.start(top_send.at[1, 4], tops.at[13], at.y_down)
    gather_total(0)
    w_hop(1, 0)
    near(1)
    far(2)
    w_hop(2, 0)
    y_left.wait_recv()
    y_far = copies.start(tops.at[12], tops.at[14], at.y_up)
    gather_total(1)
    w_hop(1, 1)
    near(2)
    w_hop(3, 0)
    w_hop(2, 1)
    w_hop(4, 0)
    gather_total(2)
    w_hop(1, 2)
    w_hop(3, 1)
    w_hop(2, 2)
    w_end(0)
    w_hop(4, 1)
    w_hop(3, 2)
    y_right.wait_recv()
    y_far.wait_recv()
    high_ref[...] = jnp.maximum(jnp.maximum(high, tops[12]), jnp.maximum(tops[13], tops[14]))
    w_end(1)
    w_hop(4, 2)
    own[2].wait()
    w_end(2)
    copies.finish()


def tail(gq, dkv, trig, top, xa, xb):
    block = (TOKENS, HEAD_DIM)
    quarter = (DEPTH // 2, SLICE, WIDTH)
    return pl.pallas_call(
        tail_kernel,
        out_shape=(
            jax.ShapeDtypeStruct((TOKENS, WIDTH), BF16),
            jax.ShapeDtypeStruct((SLICE, WIDTH), F32),
            jax.ShapeDtypeStruct((8, 128), F32),
        ),
        in_specs=[vmem_spec()] * 6,
        out_specs=(vmem_spec(),) * 3,
        scratch_shapes=[
            pltpu.VMEM((SIDE, TOKENS, WIDTH), BF16),
            pltpu.VMEM((SIDE, TOKENS, WIDTH), BF16),
            pltpu.VMEM((2, SIDE, 256, SIDE * TOKENS), BF16),
            pltpu.VMEM((DEPTH, 2) + block, BF16),
            pltpu.VMEM((4, 2) + block, BF16),
            pltpu.VMEM((4, 2) + block, BF16),
            pltpu.VMEM((4, 2) + block, BF16),
            pltpu.VMEM((4, 2) + block, BF16),
            pltpu.VMEM((TOKENS, 2 * HEAD_DIM), BF16),
            pltpu.VMEM((15, 8, 128), F32),
            pltpu.VMEM((2, 5, 8, 128), F32),
            pltpu.VMEM((2, SIDE, DEPTH // 2, 2, SLICE, WIDTH), BF16),
            pltpu.VMEM((2, SIDE) + quarter, BF16),
            pltpu.VMEM((2, 2, 2, SLICE, WIDTH), BF16),
            pltpu.VMEM((2, 2, 2, SLICE, WIDTH), BF16),
            pltpu.VMEM((2, 2) + quarter, BF16),
            pltpu.VMEM((2, 2) + quarter, BF16),
            pltpu.VMEM((DEPTH, SLICE, WIDTH), F32),
            pltpu.VMEM((4, SLICE, WIDTH), W_TYPE),
            pltpu.VMEM((4, SLICE, WIDTH), W_TYPE),
            pltpu.VMEM((4, SLICE, WIDTH), W_TYPE),
            pltpu.VMEM((4, SLICE, WIDTH), W_TYPE),
            pltpu.SemaphoreType.DMA((TAIL_COPIES,)),
            pltpu.SemaphoreType.DMA((TAIL_COPIES,)),
            pltpu.SemaphoreType.DMA((3,)),
        ],
        compiler_params=pltpu.CompilerParams(collective_id=1, has_side_effects=True, vmem_limit_bytes=40 << 20),
        name="tail",
    )(gq, dkv, trig, top, xa, xb)


def local(query_rows, key_rows, value_rows, out_grads, layer_input, doc_ids, pair_span):
    kv, xa, xb, query, out, docs, table = front(
        key_rows[0], value_rows[0], layer_input[0], query_rows[0], out_grads[0], doc_ids, jnp.asarray(trig_table())
    )
    gq, dkv, trig, top = attention(pair_span, query, out, kv, docs, table)
    rows, weight, top = tail(gq, dkv.reshape(DEPTH, 2, 2, TOKENS, HEAD_DIM), trig, top, xa, xb)
    return rows[None], weight, top[0:1, 0:2].reshape(1, 1, 2)


def solution(mesh):
    in_specs = (
        P("dp", "context", None),
        P("dp", "context", None),
        P("dp", "context", None),
        P("dp", "context", None),
        P("dp", "context", None),
        P("dp", None),
        P(),
    )
    out_specs = (P("dp", "context", None), P(("dp", "context"), None), P("dp", "context", None))
    return jax.shard_map(local, mesh=mesh, in_specs=in_specs, out_specs=out_specs, check_vma=False)
```

```python
import math

import jax
import jax.numpy as jnp
import numpy as np
from jax import lax
from jax.experimental import pallas as pl
from jax.experimental.pallas import tpu as pltpu
from jax.sharding import PartitionSpec as P

MESH = pl.DeviceIdType.MESH
THETA_BASE = 500000.0
LOG2E = 1.4426950408889634
NEG_LARGE = -1e30
HEADS, HEAD_DIM, SPAN, KEY_BLOCK = 8, 128, 96, 256
TOKENS = 2 * SPAN
SIDE, DEPTH = 4, 8
PAIRS = 2 * DEPTH
SEQ = PAIRS * TOKENS
Q_WIDTH = HEADS * HEAD_DIM
WIDTH = Q_WIDTH + 2 * HEAD_DIM
LANES = HEADS * SPAN
F32, BF16 = jnp.float32, jnp.bfloat16
W_TYPE = BF16


class Place:
    def __init__(self):
        dp, context = lax.axis_index("dp"), lax.axis_index("context")
        self.context = context
        self.y, self.x = dp // SIDE, dp % SIDE
        self.z, self.core = context // 2, context % 2
        z_next, z_prev = (self.z + 1) % DEPTH, (self.z + DEPTH - 1) % DEPTH
        self.z_up, self.z_down = (dp, z_next * 2 + self.core), (dp, z_prev * 2 + self.core)
        self.x_up = (self.y * SIDE + (self.x + 1) % SIDE, context)
        self.x_down = (self.y * SIDE + (self.x + SIDE - 1) % SIDE, context)
        self.y_up = ((self.y + 1) % SIDE * SIDE + self.x, context)
        self.y_down = ((self.y + SIDE - 1) % SIDE * SIDE + self.x, context)
        self.sibling = (dp, context + 1 - 2 * self.core)
        self.rings = ((self.x, self.x_up, self.x_down), (self.y, self.y_up, self.y_down))

    def along_z(self, hops):
        return (lax.axis_index("dp"), (self.z + hops) % DEPTH * 2 + self.core)

    def greet(self, *more):
        barrier = pltpu.get_barrier_semaphore()
        peers = (self.z_up, self.z_down, self.x_up, self.x_down, self.y_up, self.y_down, self.sibling) + more
        for peer in peers:
            pl.semaphore_signal(barrier, inc=1, device_id=peer, device_id_type=MESH)
        pl.semaphore_wait(barrier, len(peers))


class Copies:
    def __init__(self, send, recv):
        self.send, self.recv, self.all = send, recv, []

    def start(self, src, dst, device):
        i = len(self.all)
        copy = pltpu.make_async_remote_copy(
            src_ref=src, dst_ref=dst, send_sem=self.send.at[i], recv_sem=self.recv.at[i],
            device_id=device, device_id_type=MESH,
        )
        copy.start()
        self.all.append(copy)
        return copy

    def finish(self):
        for copy in self.all:
            copy.wait_send()


FRONT_COPIES = 62


def front_kernel(k_ref, v_ref, x_ref, *refs):
    staged, (kv_ref, xa_ref, xb_ref), held, (transit, send, recv, local) = refs[:4], refs[4:7], refs[7:11], refs[11:]
    at = Place()
    at.greet()
    copies = Copies(send, recv)
    planes = (k_ref, v_ref)
    own = [pltpu.make_async_copy(planes[p], kv_ref.at[at.context, p], local.at[p]) for p in range(2)]
    up, down, side = {}, {}, []
    for p in range(2):
        dst = kv_ref.at[at.context, p]
        up[1, p] = copies.start(planes[p], dst, at.z_up)
        down[1, p] = copies.start(planes[p], dst, at.z_down)
    for p in range(2):
        side.append(copies.start(planes[p], kv_ref.at[at.context, p], at.sibling))

    def column(yy, xx, part):
        return pl.ds(pl.multiple_of(((yy * SIDE + xx) * 2 + part) * 256, 256), 256)

    columns_of = (lambda dest, j: column(j, dest, 0), lambda dest, j: column(dest, j, 1))
    outs = (xa_ref, xb_ref)
    far, near = {}, []
    for g, (n, right, left) in enumerate(at.rings):
        dest = (n + 2) % SIDE
        for j in range(2):
            far[g, 0, j] = copies.start(x_ref.at[:, columns_of[g](dest, j)], transit.at[g, 0, j], right)
            far[g, 1, j] = copies.start(x_ref.at[:, columns_of[g](dest, j + 2)], transit.at[g, 1, j], left)
    for g, (n, right, left) in enumerate(at.rings):
        for j in range(SIDE):
            dst = outs[g].at[n, :, j * 256:(j + 1) * 256]
            near.append(copies.start(x_ref.at[:, columns_of[g]((n + 1) % SIDE, j)], dst, right))
            near.append(copies.start(x_ref.at[:, columns_of[g]((n + 3) % SIDE, j)], dst, left))
    for g, (n, right, left) in enumerate(at.rings):
        for j in range(SIDE):
            src = x_ref.at[:, columns_of[g](n, j)]
            own.append(pltpu.make_async_copy(src, outs[g].at[n, :, j * 256:(j + 1) * 256], local.at[len(own)]))
    def relay_inputs():
        for g, (n, right, left) in enumerate(at.rings):
            for j in range(2):
                far[g, 0, j].wait_recv()
                dst = outs[g].at[(n + 3) % SIDE, :, j * 256:(j + 1) * 256]
                near.append(copies.start(transit.at[g, 0, j], dst, right))
                far[g, 1, j].wait_recv()
                dst = outs[g].at[(n + 1) % SIDE, :, (j + 2) * 256:(j + 3) * 256]
                near.append(copies.start(transit.at[g, 1, j], dst, left))

    for src, dst in zip(staged, held):
        own.append(pltpu.make_async_copy(src, dst, local.at[len(own)]))
    for copy in own:
        copy.start()

    for t in range(1, 5):
        if t == 3:
            relay_inputs()
        for p in range(2):
            if (t, p) in up:
                up[t, p].wait_recv()
                block = kv_ref.at[(at.z + DEPTH - t) % DEPTH * 2 + at.core, p]
                if t < 3 or (t == 3 and p == 0):
                    up[t + 1, p] = copies.start(block, block, at.z_up)
                side.append(copies.start(block, block, at.sibling))
            if (t, p) in down:
                down[t, p].wait_recv()
                block = kv_ref.at[(at.z + t) % DEPTH * 2 + at.core, p]
                if t < 3 or (t == 3 and p == 1):
                    down[t + 1, p] = copies.start(block, block, at.z_down)
                side.append(copies.start(block, block, at.sibling))
    for copy in side + near:
        copy.wait_recv()
    for copy in own:
        copy.wait()
    copies.finish()


def hbm_spec():
    return pl.BlockSpec(memory_space=pltpu.HBM)


def vmem_spec():
    return pl.BlockSpec(memory_space=pltpu.VMEM)


def front(keys, values, inputs, *staged):
    half = inputs.shape[1] // 8
    return pl.pallas_call(
        front_kernel,
        out_shape=(
            jax.ShapeDtypeStruct((PAIRS, 2, TOKENS, HEAD_DIM), BF16),
            jax.ShapeDtypeStruct((SIDE, TOKENS, half), BF16),
            jax.ShapeDtypeStruct((SIDE, TOKENS, half), BF16),
        ) + tuple(jax.ShapeDtypeStruct(a.shape, a.dtype) for a in staged),
        in_specs=[hbm_spec()] * 7,
        out_specs=(vmem_spec(),) * 7,
        scratch_shapes=[
            pltpu.VMEM((2, 2, 2, TOKENS, 256), BF16),
            pltpu.SemaphoreType.DMA((FRONT_COPIES,)),
            pltpu.SemaphoreType.DMA((FRONT_COPIES,)),
            pltpu.SemaphoreType.DMA((14,)),
        ],
        compiler_params=pltpu.CompilerParams(collective_id=0, has_side_effects=True, vmem_limit_bytes=12 << 20),
        name="front",
    )(*(pltpu.with_memory_space_constraint(a, pltpu.HBM) for a in (keys, values, inputs) + staged))


def trig_table():
    inverse_freq = THETA_BASE ** (-2.0 * np.arange(HEAD_DIM // 2) / HEAD_DIM)
    freq = np.concatenate([inverse_freq, inverse_freq])
    sign = np.concatenate([np.ones(HEAD_DIM // 2), -np.ones(HEAD_DIM // 2)])
    base = (np.arange(2 * PAIRS) * SPAN)[:, None] * freq[None, :]
    step = np.arange(SPAN)[:, None] * freq[None, :]
    parts = [np.cos(base), np.sin(base) * sign, np.cos(step), np.sin(step) * sign]
    return np.concatenate(parts).astype(np.float32)


def fold8(x, op):
    out = x[0:8]
    for r in range(8, x.shape[0], 8):
        out = op(out, x[r:r + 8])
    return out


def attention_kernel(
    pair_ref, query_ref, out_ref, kv_ref, docs_ref, table_ref,
    gq_ref, dkv_ref, trig_ref, top_ref,
    k_pos, v_pos, qs, gs, s_scr, d_scr, top_scr, dk_acc, dv_acc, dq_acc,
):
    me = lax.axis_index("context")
    scale = 1.0 / math.sqrt(HEAD_DIM)

    def stored_spans():
        for p in range(PAIRS):
            low = pair_ref[p]
            for half, s in ((0, low), (1, 2 * PAIRS - 1 - low)):
                yield p, pl.ds(half * SPAN, SPAN), pl.ds(pl.multiple_of(s * SPAN, 32), SPAN)

    for p, rows, at in stored_spans():
        k_pos[at, :] = kv_ref[p, 0, rows, :]
        v_pos[at, :] = kv_ref[p, 1, rows, :]
    dk_acc[...] = jnp.zeros_like(dk_acc)
    dv_acc[...] = jnp.zeros_like(dv_acc)
    docs = docs_ref[...]
    starts = [
        jnp.sum(jnp.where(docs < d, 1.0, 0.0), axis=1, keepdims=True).astype(jnp.int32) for d in range(1, 8)
    ]
    lane = lax.broadcasted_iota(jnp.int32, (1, LANES), 1)
    row = lane - SPAN * ((lane * 683) >> 16)

    ds_top = jnp.zeros((8, LANES), F32)
    own_low = pair_ref[me]
    for half in range(2):
        s = own_low if half == 0 else 2 * PAIRS - 1 - own_low
        first = half * SPAN
        for h in range(HEADS):
            head = slice(h * HEAD_DIM, (h + 1) * HEAD_DIM)
            qs[h * SPAN:(h + 1) * SPAN, :] = query_ref[first:first + SPAN, head]
            gs[h * SPAN:(h + 1) * SPAN, :] = out_ref[first:first + SPAN, head]
        q_pos = row + s * SPAN
        start = jnp.zeros((1, LANES), jnp.int32)
        for first_of in starts:
            start = jnp.where(first_of <= q_pos, jnp.maximum(start, first_of), start)
        lo = jnp.min(start) // KEY_BLOCK
        hi = (s * SPAN + SPAN - 1) // KEY_BLOCK + 1
        dq_acc[...] = jnp.zeros_like(dq_acc)

        def block_rows(b):
            return pl.ds(pl.multiple_of(b * KEY_BLOCK, KEY_BLOCK), KEY_BLOCK)

        def weigh(b, state):
            top, total, weighted = state
            sc = lax.dot_general(
                k_pos[block_rows(b), :], qs[...], (((1,), (1,)), ((), ())), preferred_element_type=F32
            )
            dp = lax.dot_general(
                v_pos[block_rows(b), :], gs[...], (((1,), (1,)), ((), ())), preferred_element_type=F32
            )
            d_scr[b] = dp
            key_pos = b * KEY_BLOCK + lax.broadcasted_iota(jnp.int32, (KEY_BLOCK, LANES), 0)
            sc = jnp.where((key_pos <= q_pos) & (key_pos >= start), sc, NEG_LARGE)
            new_top = jnp.maximum(top, jnp.max(fold8(sc, jnp.maximum), axis=0, keepdims=True))
            e = jnp.exp2((sc - new_top) * (scale * LOG2E))
            s_scr[b] = e
            top_scr[b] = new_top
            factor = jnp.exp2((top - new_top) * (scale * LOG2E))
            return new_top, total * factor + fold8(e, jnp.add), weighted * factor + fold8(e * dp, jnp.add)

        zero = jnp.zeros((8, LANES), F32)
        top, total, weighted = lax.fori_loop(lo, hi, weigh, (jnp.full((1, LANES), NEG_LARGE, F32), zero, zero))
        inverse = 1.0 / jnp.sum(total, axis=0, keepdims=True)
        delta = jnp.sum(weighted, axis=0, keepdims=True) * inverse

        def grads(b, high):
            at = block_rows(b)
            p = s_scr[b] * (jnp.exp2((top_scr[b] - top) * (scale * LOG2E)) * inverse)
            ds = p * (d_scr[b] - delta)
            p16, ds16 = p.astype(BF16), ds.astype(BF16)
            dv_acc[at, :] += jnp.dot(p16, gs[...], preferred_element_type=F32)
            dk_acc[at, :] += jnp.dot(ds16, qs[...], preferred_element_type=F32)
            dq_acc[...] += lax.dot_general(
                k_pos[at, :], ds16, (((0,), (0,)), ((), ())), preferred_element_type=F32
            )
            return jnp.maximum(high, fold8(jnp.abs(ds), jnp.maximum))

        ds_top = lax.fori_loop(lo, hi, grads, ds_top)
        cos_a, sin_a = table_ref[pl.ds(s, 1), :], table_ref[pl.ds(2 * PAIRS + s, 1), :]
        cos_b, sin_b = table_ref[4 * PAIRS:4 * PAIRS + SPAN, :], table_ref[4 * PAIRS + SPAN:, :]
        cosine = cos_a * cos_b - sin_a * sin_b
        sine = sin_a * cos_b + cos_a * sin_b
        trig_ref[0, first:first + SPAN, :] = cosine
        trig_ref[1, first:first + SPAN, :] = sine
        dq = dq_acc[...].T * scale
        for h in range(HEADS):
            v = dq[h * SPAN:(h + 1) * SPAN, :]
            turned = v * cosine + pltpu.roll(v, HEAD_DIM // 2, 1) * sine
            gq_ref[first:first + SPAN, h * HEAD_DIM:(h + 1) * HEAD_DIM] = turned.astype(BF16)

    for p, rows, at in stored_spans():
        dkv_ref[p, 0, rows, :] = dk_acc[at, :].astype(dkv_ref.dtype)
        dkv_ref[p, 1, rows, :] = dv_acc[at, :].astype(dkv_ref.dtype)
    out_top = jnp.max(fold8(jnp.abs(out_ref[...].astype(F32)), jnp.maximum))
    column = lax.broadcasted_iota(jnp.int32, top_ref.shape, 1)
    top_ref[...] = jnp.where(column == 0, out_top, jnp.max(ds_top))


def attention(pair_span, query, out, kv, docs, table):
    return pl.pallas_call(
        attention_kernel,
        out_shape=(
            jax.ShapeDtypeStruct((TOKENS, Q_WIDTH), BF16),
            jax.ShapeDtypeStruct((PAIRS, 2, TOKENS, HEAD_DIM), BF16),
            jax.ShapeDtypeStruct((2, TOKENS, HEAD_DIM), F32),
            jax.ShapeDtypeStruct((8, 128), F32),
        ),
        in_specs=[pl.BlockSpec(memory_space=pltpu.SMEM)] + [vmem_spec()] * 5,
        out_specs=(vmem_spec(),) * 4,
        scratch_shapes=[
            pltpu.VMEM((SEQ, HEAD_DIM), BF16),
            pltpu.VMEM((SEQ, HEAD_DIM), BF16),
            pltpu.VMEM((LANES, HEAD_DIM), BF16),
            pltpu.VMEM((LANES, HEAD_DIM), BF16),
            pltpu.VMEM((SEQ // KEY_BLOCK, KEY_BLOCK, LANES), F32),
            pltpu.VMEM((SEQ // KEY_BLOCK, KEY_BLOCK, LANES), F32),
            pltpu.VMEM((SEQ // KEY_BLOCK, 1, LANES), F32),
            pltpu.VMEM((SEQ, HEAD_DIM), F32),
            pltpu.VMEM((SEQ, HEAD_DIM), F32),
            pltpu.VMEM((HEAD_DIM, LANES), F32),
        ],
        compiler_params=pltpu.CompilerParams(vmem_limit_bytes=40 << 20),
        name="attention",
    )(pair_span, query, out, kv, docs, table)


TAIL_COPIES = 180
SLICE = 32
CHUNKS = ((0, 512), (512, 512), (1024, 256))


def tail_kernel(
    gq_ref, dkv_ref, trig_ref, top_ref, xa_ref, xb_ref, rows_ref, w_ref, high_ref,
    gx, gy, turned, sib, up_send, up_recv, down_send, down_recv, gkv, tops, top_send,
    partial, partial_sib, far_send, far_recv, near_send, near_recv, total,
    w_up_send, w_up_recv, w_down_send, w_down_recv, last_send, last_recv, send, recv, local,
):
    at = Place()
    at.greet(*(at.along_z(k) for k in range(2, DEPTH - 1)))
    copies = Copies(send, recv)
    gathered, inputs = (gx, gy), (xa_ref, xb_ref)
    q_cols = pl.ds(0, Q_WIDTH)

    from_left, from_right, spreading = {}, {}, {c: [] for c in range(len(CHUNKS))}

    def spread(c):
        first, width = CHUNKS[c]
        src = gkv if first == Q_WIDTH else gq_ref.at[:, pl.ds(first, width)]
        for g, (n, right, left) in enumerate(at.rings):
            dst = gathered[g].at[n, :, pl.ds(first, width)]
            from_left[g, c] = copies.start(src, dst, right)
            from_right[g, c] = copies.start(src, dst, left)

    def relay(c):
        first, width = CHUNKS[c]
        for g, (n, right, left) in enumerate(at.rings):
            from_left[g, c].wait_recv()
            block = gathered[g].at[(n + 3) % SIDE, :, pl.ds(first, width // 2)]
            spreading[c].append(copies.start(block, block, right))
            from_right[g, c].wait_recv()
            block = gathered[g].at[(n + 1) % SIDE, :, pl.ds(first + width // 2, width // 2)]
            spreading[c].append(copies.start(block, block, left))

    sides = {}

    def part(dest, p):
        return dkv_ref[dest, at.core, p].astype(F32) + sib[dest, p].astype(F32)

    ups, downs, up_tops, down_tops = {}, {}, {}, {}

    def key_value_hop(t, high):
        shift_up, shift_down = 5 - t, 3 + t
        for shift in sorted({shift_up, shift_down}):
            sides[shift].wait_recv()
        for p in range(2):
            for up in (True, False):
                if t == 1 and up != (p == 0):
                    continue
                moves, sent, got = (ups, up_send, up_recv) if up else (downs, down_send, down_recv)
                value = part((at.z + (shift_up if up else shift_down)) % DEPTH, p)
                if (t - 1, p) in moves:
                    moves[t - 1, p].wait_recv()
                    value = value + got[t - 2, p].astype(F32)
                sent[t - 1, p] = value.astype(BF16)
                moves[t, p] = copies.start(sent.at[t - 1, p], got.at[t - 1, p], at.z_up if up else at.z_down)
        if t > 1:
            up_tops[t - 1].wait_recv()
            down_tops[t - 1].wait_recv()
            top_send[0, t - 1] = jnp.maximum(high, tops[2 * t - 3])
            top_send[1, t - 1] = jnp.maximum(high, tops[2 * t - 2])
        else:
            top_send[0, 0] = high
            top_send[1, 0] = high
        up_tops[t] = copies.start(top_send.at[0, t - 1], tops.at[2 * t - 1], at.z_up)
        down_tops[t] = copies.start(top_send.at[1, t - 1], tops.at[2 * t], at.z_down)

    crossing, fars, nears, w_ups, w_downs = {}, {}, {}, {}, {}
    ring = (at.rings[1], at.rings[0])
    low, upper = slice(0, 2), slice(2, 4)

    def turn(g):
        for j in range(SIDE):
            block = inputs[g][:, :, j * 256:(j + 1) * 256].reshape(SIDE * TOKENS, 256)
            turned[g, j] = block.T

    def multiply(c):
        first, width = CHUNKS[c]
        cols = pl.ds(first, width)
        for copy in spreading[c]:
            copy.wait_recv()
        for hop in (2, 1, 3, 0):
            for g in range(2):
                dest = (ring[g][0] + hop) % SIDE
                rows = gathered[g][:, :, cols].reshape(SIDE * TOKENS, width)
                product = jnp.dot(turned[g, dest], rows, preferred_element_type=F32)
                partial[g, dest, :, :, :, cols] = product.astype(BF16).reshape(DEPTH // 2, 2, SLICE, width)
                crossing[g, hop, c] = copies.start(
                    partial.at[g, dest, :, 1 - at.core, :, cols], partial_sib.at[g, dest, :, :, cols], at.sibling
                )

    def w_part(g, dest, rows, cols):
        return partial[g, dest, rows, at.core, :, cols].astype(F32) + partial_sib[g, dest, rows, :, cols].astype(F32)

    def far(c):
        cols = pl.ds(*CHUNKS[c])
        for g in range(2):
            n, right, left = ring[g]
            dest = (n + 2) % SIDE
            crossing[g, 2, c].wait_recv()
            for arm, rows, device in ((0, low, right), (1, upper, left)):
                far_send[g, arm, :, :, cols] = w_part(g, dest, rows, cols).astype(BF16)
                fars[g, arm, c] = copies.start(
                    far_send.at[g, arm, :, :, cols], far_recv.at[g, arm, :, :, cols], device
                )

    def near(c):
        cols = pl.ds(*CHUNKS[c])
        for g in range(2):
            n, right, left = ring[g]
            for arm, hop, device in ((0, 1, right), (1, 3, left)):
                dest = (n + hop) % SIDE
                crossing[g, hop, c].wait_recv()
                joined, alone = (low, upper) if arm == 0 else (upper, low)
                near_send[g, arm, alone, :, cols] = w_part(g, dest, alone, cols).astype(BF16)
                fars[g, arm, c].wait_recv()
                value = w_part(g, dest, joined, cols) + far_recv[g, arm, :, :, cols].astype(F32)
                near_send[g, arm, joined, :, cols] = value.astype(BF16)
                nears[g, arm, c] = copies.start(
                    near_send.at[g, arm, :, :, cols], near_recv.at[g, arm, :, :, cols], device
                )

    def gather_total(c):
        cols = pl.ds(*CHUNKS[c])
        for g in range(2):
            crossing[g, 0, c].wait_recv()
            value = w_part(g, ring[g][0], slice(0, 4), cols)
            for arm in range(2):
                nears[g, arm, c].wait_recv()
                value = value + near_recv[g, arm, :, :, cols].astype(F32)
            total[4 * g:4 * g + 4, :, cols] = value

    def w_hop(t, c):
        first, width = CHUNKS[c]
        cols, half = pl.ds(first, width), width // 2
        sides_of = (pl.ds(first, half), pl.ds(first + half, half))
        for up in (True, False):
            moves, sent, got, device = (
                (w_ups, w_up_send, w_up_recv, at.z_up) if up else (w_downs, w_down_send, w_down_recv, at.z_down)
            )
            dest = (at.z + (5 - t if up else 3 + t)) % DEPTH
            joined, alone = sides_of if up else sides_of[::-1]
            if t == 1:
                sent[0, :, joined] = total[dest, :, joined].astype(W_TYPE)
                moves[1, c] = copies.start(sent.at[0, :, joined], got.at[0, :, joined], device)
                continue
            if t == 2:
                sent[1, :, alone] = total[dest, :, alone].astype(W_TYPE)
                moves[1, c].wait_recv()
                sent[1, :, joined] = (total[dest, :, joined] + got[0, :, joined].astype(F32)).astype(W_TYPE)
            else:
                moves[t - 1, c].wait_recv()
                sent[t - 1, :, cols] = (total[dest, :, cols] + got[t - 2, :, cols].astype(F32)).astype(W_TYPE)
            moves[t, c] = copies.start(sent.at[t - 1, :, cols], got.at[t - 1, :, cols], device)

    def w_end(c):
        cols = pl.ds(*CHUNKS[c])
        w_ups[4, c].wait_recv()
        w_downs[4, c].wait_recv()
        w_ref[:, cols] = total[at.z, :, cols] + w_up_recv[3, :, cols].astype(F32) + w_down_recv[3, :, cols].astype(F32)

    lasts = {}

    def direct(c):
        first, width = CHUNKS[c]
        cols, kept = pl.ds(first, width), pl.ds(first - CHUNKS[1][0], width)
        for k in (4, 3, 5, 2, 6, 1, 7):
            last_send[k, :, kept] = total[(at.z + k) % DEPTH, :, cols].astype(W_TYPE)
            lasts[c, k] = copies.start(last_send.at[k, :, kept], last_recv.at[k, :, kept], at.along_z(k))

    def direct_end(c):
        first, width = CHUNKS[c]
        cols, kept = pl.ds(first, width), pl.ds(first - CHUNKS[1][0], width)
        value = total[at.z, :, cols]
        for k in (1, 7, 2, 6, 3, 5, 4):
            lasts[c, k].wait_recv()
            value = value + last_recv[k, :, kept].astype(F32)
        w_ref[:, cols] = value

    spread(0)
    side_top = copies.start(top_ref, tops.at[0], at.sibling)
    for shift in (4, 5, 3, 6, 2, 7, 1, 0):
        dest = (at.z + shift) % DEPTH
        sides[shift] = copies.start(dkv_ref.at[dest, 1 - at.core], sib.at[dest], at.sibling)
    own = [
        pltpu.make_async_copy(gq_ref, gathered[g].at[n, :, q_cols], local.at[g])
        for g, (n, right, left) in enumerate(at.rings)
    ]
    own.append(pltpu.make_async_copy(gq_ref, rows_ref.at[:, q_cols], local.at[2]))
    for copy in own:
        copy.start()
    side_top.wait_recv()
    high = jnp.maximum(top_ref[...], tops[0])
    key_value_hop(1, high)
    spread(1)
    turn(0)
    key_value_hop(2, high)
    turn(1)
    relay(0)
    key_value_hop(3, high)
    relay(1)
    key_value_hop(4, high)
    for copy in own[0:2]:
        copy.wait()
    multiply(0)

    scale = 1.0 / math.sqrt(HEAD_DIM)
    sides[0].wait_recv()
    sums = []
    for p in range(2):
        ups[4, p].wait_recv()
        downs[4, p].wait_recv()
        sums.append(part(at.z, p) + up_recv[3, p].astype(F32) + down_recv[3, p].astype(F32))
    gk = sums[0] * scale
    gk = gk * trig_ref[0] + pltpu.roll(gk, HEAD_DIM // 2, 1) * trig_ref[1]
    gkv[:, 0:HEAD_DIM] = gk.astype(BF16)
    gkv[:, HEAD_DIM:] = sums[1].astype(BF16)
    spread(2)
    rows_ref[:, Q_WIDTH:] = gkv[...]
    for g, (n, right, left) in enumerate(at.rings):
        gathered[g][n, :, Q_WIDTH:] = gkv[...]
    up_tops[4].wait_recv()
    down_tops[4].wait_recv()
    high = jnp.maximum(jnp.maximum(high, tops[7]), tops[8])
    top_send[0, 4] = high
    x_left = copies.start(top_send.at[0, 4], tops.at[9], at.x_up)
    x_right = copies.start(top_send.at[0, 4], tops.at[10], at.x_down)
    far(0)
    multiply(1)
    far(1)
    near(0)
    relay(2)
    x_left.wait_recv()
    x_far = copies.start(tops.at[9], tops.at[11], at.x_up)
    near(1)
    multiply(2)
    far(2)
    gather_total(0)
    w_hop(1, 0)
    x_right.wait_recv()
    x_far.wait_recv()
    high = jnp.maximum(jnp.maximum(high, tops[9]), jnp.maximum(tops[10], tops[11]))
    top_send[1, 4] = high
    y_left = copies.start(top_send.at[1, 4], tops.at[12], at.y_up)
    y_right = copies.start(top_send.at[1, 4], tops.at[13], at.y_down)
    near(2)
    w_hop(2, 0)
    gather_total(1)
    direct(1)
    w_hop(3, 0)
    y_left.wait_recv()
    y_far = copies.start(tops.at[12], tops.at[14], at.y_up)
    gather_total(2)
    direct(2)
    w_hop(4, 0)
    y_right.wait_recv()
    y_far.wait_recv()
    high_ref[...] = jnp.maximum(jnp.maximum(high, tops[12]), jnp.maximum(tops[13], tops[14]))
    w_end(0)
    direct_end(1)
    direct_end(2)
    own[2].wait()
    copies.finish()


def tail(gq, dkv, trig, top, xa, xb):
    block = (TOKENS, HEAD_DIM)
    quarter = (DEPTH // 2, SLICE, WIDTH)
    return pl.pallas_call(
        tail_kernel,
        out_shape=(
            jax.ShapeDtypeStruct((TOKENS, WIDTH), BF16),
            jax.ShapeDtypeStruct((SLICE, WIDTH), F32),
            jax.ShapeDtypeStruct((8, 128), F32),
        ),
        in_specs=[vmem_spec()] * 6,
        out_specs=(vmem_spec(),) * 3,
        scratch_shapes=[
            pltpu.VMEM((SIDE, TOKENS, WIDTH), BF16),
            pltpu.VMEM((SIDE, TOKENS, WIDTH), BF16),
            pltpu.VMEM((2, SIDE, 256, SIDE * TOKENS), BF16),
            pltpu.VMEM((DEPTH, 2) + block, BF16),
            pltpu.VMEM((4, 2) + block, BF16),
            pltpu.VMEM((4, 2) + block, BF16),
            pltpu.VMEM((4, 2) + block, BF16),
            pltpu.VMEM((4, 2) + block, BF16),
            pltpu.VMEM((TOKENS, 2 * HEAD_DIM), BF16),
            pltpu.VMEM((15, 8, 128), F32),
            pltpu.VMEM((2, 5, 8, 128), F32),
            pltpu.VMEM((2, SIDE, DEPTH // 2, 2, SLICE, WIDTH), BF16),
            pltpu.VMEM((2, SIDE) + quarter, BF16),
            pltpu.VMEM((2, 2, 2, SLICE, WIDTH), BF16),
            pltpu.VMEM((2, 2, 2, SLICE, WIDTH), BF16),
            pltpu.VMEM((2, 2) + quarter, BF16),
            pltpu.VMEM((2, 2) + quarter, BF16),
            pltpu.VMEM((DEPTH, SLICE, WIDTH), F32),
            pltpu.VMEM((4, SLICE, WIDTH), W_TYPE),
            pltpu.VMEM((4, SLICE, WIDTH), W_TYPE),
            pltpu.VMEM((4, SLICE, WIDTH), W_TYPE),
            pltpu.VMEM((4, SLICE, WIDTH), W_TYPE),
            pltpu.VMEM((DEPTH, SLICE, WIDTH - CHUNKS[1][0]), W_TYPE),
            pltpu.VMEM((DEPTH, SLICE, WIDTH - CHUNKS[1][0]), W_TYPE),
            pltpu.SemaphoreType.DMA((TAIL_COPIES,)),
            pltpu.SemaphoreType.DMA((TAIL_COPIES,)),
            pltpu.SemaphoreType.DMA((3,)),
        ],
        compiler_params=pltpu.CompilerParams(collective_id=1, has_side_effects=True, vmem_limit_bytes=40 << 20),
        name="tail",
    )(gq, dkv, trig, top, xa, xb)


def local(query_rows, key_rows, value_rows, out_grads, layer_input, doc_ids, pair_span):
    kv, xa, xb, query, out, docs, table = front(
        key_rows[0], value_rows[0], layer_input[0], query_rows[0], out_grads[0], doc_ids, jnp.asarray(trig_table())
    )
    gq, dkv, trig, top = attention(pair_span, query, out, kv, docs, table)
    rows, weight, top = tail(gq, dkv.reshape(DEPTH, 2, 2, TOKENS, HEAD_DIM), trig, top, xa, xb)
    return rows[None], weight, top[0:1, 0:2].reshape(1, 1, 2)


def solution(mesh):
    in_specs = (
        P("dp", "context", None),
        P("dp", "context", None),
        P("dp", "context", None),
        P("dp", "context", None),
        P("dp", "context", None),
        P("dp", None),
        P(),
    )
    out_specs = (P("dp", "context", None), P(("dp", "context"), None), P("dp", "context", None))
    return jax.shard_map(local, mesh=mesh, in_specs=in_specs, out_specs=out_specs, check_vma=False)
```
